256 devices in a mesh: ctx: 64 (over z, x, y_hi), fft: 4 (over y_lo, core).
Axes of the slice: x: 4, y: 4 (y_hi: 2, y_lo: 2; y = y_hi * 2 + y_lo), z: 8, core: 2. Of those that a mesh axis runs over, the one named last changes fastest.
Arguments:
- tokens: bfloat16 [32768, 2048], P('ctx'), may hold values from -6 to 6
- w_in: bfloat16 [2048, 3, 2048], P(None, None, 'fft'), may hold values from -0.125 to 0.125
- short_taps: float32 [7, 384], replicated, may hold values from -2 to 2
- long_filter: float32 [32768, 128], P('ctx'), may hold values from -0.03125 to 0.03125
- skip_gain: float32 [2048], replicated, may hold values from -4 to 4
- w_out: bfloat16 [2048, 2048], P('fft'), may hold values from -0.125 to 0.125
Outputs:
- mixed: bfloat16 [32768, 2048], P(('ctx', 'fft'))
The draws below stay inside these ranges and needn't reach their ends.
All inputs are finite; a program needn't handle non-finite values.
Results may differ from the reference program's by a relative error of at most 0.014.
Values may be sent and summed in bfloat16 or wider, within the bound.
A program may use at most 128 MiB of HBM per device.

```python
import jax
import jax.numpy as jnp
from jax import lax

D = 2048
GROUPS = 128
GS = 16
TAPS = 7
SEQ = 32768


def steps_of(own_key, extent, cuts, low, high):
    level = 1.0
    for axis_at, parts in cuts:
        steps = jax.random.uniform(jax.random.fold_in(jax.random.fold_in(own_key, 6), axis_at), (parts,), jnp.float32, low / len(cuts), high / len(cuts))
        level = level * jnp.repeat(jnp.exp(steps), extent[axis_at] // parts).reshape((-1,) + (1,) * (len(extent) - 1 - axis_at))
    return level


def scatter_about(stream_key, dims, spread, limit, shards=(), held_as=jnp.bfloat16):
    factor_of = steps_of(stream_key, dims, shards, -0.22, 0.18) if shards else 1.0
    drawn = jax.random.normal(stream_key, dims, jnp.float32) * spread * factor_of
    return jnp.minimum(jnp.maximum(drawn, -limit), limit).astype(held_as)


def setup_inputs(seed: int = 0) -> dict:
    keys = jax.random.split(jax.random.key(seed), 7)
    return {
        "tokens": scatter_about(keys[0], (SEQ, D), 1.0, 6.0, ((0, 64),)),
        "w_in": scatter_about(keys[1], (D, 3, D), D ** -0.5, 0.125, ((2, 4),)),
        "short_taps": scatter_about(keys[2], (TAPS, 3 * GROUPS), TAPS ** -0.5, 2.0, (), jnp.float32),
        "long_filter": scatter_about(keys[3], (SEQ, GROUPS), SEQ ** -0.5, 0.03125, ((0, 64),), jnp.float32),
        "skip_gain": scatter_about(keys[4], (D,), 1.0, 4.0, (), jnp.float32),
        "w_out": scatter_about(keys[5], (D, D), D ** -0.5, 0.125, ((0, 4),)),
    }


def reference(tokens, w_in, short_taps, long_filter, skip_gain, w_out):
    proj = jnp.dot(tokens, w_in.reshape(D, 3 * D), preferred_element_type=jnp.float32).astype(jnp.bfloat16)
    taps_full = jnp.repeat(short_taps, GS, axis=1)
    widened = proj.astype(jnp.float32)
    padded = jnp.concatenate([jnp.zeros((TAPS - 1, 3 * D), jnp.float32), widened], axis=0)
    feat = jnp.zeros_like(widened)
    for shift_count in range(TAPS):
        start = TAPS - 1 - shift_count
        feat = feat + taps_full[shift_count] * padded[start:start + SEQ]
    feat = feat.astype(jnp.bfloat16)
    query = feat[:, :D].astype(jnp.float32)
    mixed_in = feat[:, D:2 * D].astype(jnp.float32) * feat[:, 2 * D:].astype(jnp.float32)

    def per_group(group):
        filt = lax.dynamic_slice_in_dim(long_filter, group, 1, 1)[:, 0]
        block = lax.dynamic_slice_in_dim(mixed_in, group * GS, GS, 1)
        spectrum = jnp.fft.rfft(block, n=2 * SEQ, axis=0) * jnp.fft.rfft(filt, n=2 * SEQ)[:, None]
        return jnp.fft.irfft(spectrum, n=2 * SEQ, axis=0)[:SEQ].astype(jnp.float32)

    conv = lax.map(per_group, jnp.arange(GROUPS, dtype=jnp.int32))
    conv = conv.transpose(1, 0, 2).reshape(SEQ, D)
    gated = (query * (conv + skip_gain * mixed_in)).astype(jnp.bfloat16)
    return jnp.dot(gated, w_out, preferred_element_type=jnp.float32).astype(jnp.bfloat16)
```

```python
import functools
import math

import jax
import jax.numpy as jnp
import numpy as np
from jax import lax
from jax.experimental import pallas as pl
from jax.experimental.pallas import tpu as pltpu
from jax.sharding import PartitionSpec as P

MESH = pl.DeviceIdType.MESH
F32 = jnp.float32
BF16 = jnp.bfloat16
RIM = 8


def tables(n_ctx, tok_len, stretch):
    blocks = np.arange(n_ctx)
    lags = np.arange(tok_len)
    odd = 2 * blocks + 1
    angle = (odd[:, None] * blocks[None, :] % (4 * n_ctx)) * (2.0 * math.pi / (4 * n_ctx))
    eye = np.eye(stretch)
    over_blocks = np.concatenate([np.cos(angle), -np.sin(angle)], axis=0)
    spread = np.kron(over_blocks, eye)
    turn = (odd[:, None] * lags[None, :]) * (2.0 * math.pi / (4 * n_ctx * tok_len))
    turns = np.stack([np.cos(turn), -np.sin(turn)])
    inner = (lags[:, None] * lags[None, :] % tok_len) * (2.0 * math.pi / tok_len)
    waves = np.concatenate([np.cos(inner), np.sin(inner)], axis=0)
    return (
        over_blocks.astype(np.float32),
        spread.astype(np.float32).astype(jnp.bfloat16),
        turns.astype(np.float32),
        waves.astype(np.float32).astype(jnp.bfloat16),
    )


def dot(a, b, **kw):
    return jnp.dot(a, b, preferred_element_type=F32, **kw)


def kernel(
    n_ctx, n_fft, group_size,
    tok_hbm, w_hbm, taps_hbm, filt_hbm, gain_hbm, wout_hbm, over_hbm, spread_hbm, turns_hbm, waves_hbm,
    out_ref,
    tok, w, taps_in, filt, gain_in, wout, over, spread, turns, waves,
    spread_t, proj, mixed, query, send, recv, filt_send, filt_recv,
    signal, stage, lhs, spec, back, send2, recv2, gated, kept,
    pair_send, pair_recv, cross_send, cross_recv,
    load_sem, rim_send_sem, rim_recv_sem, filt_send_sem, filt_recv_sem,
    go_send_sem, go_recv_sem, come_send_sem, come_recv_sem,
    pair_send_sem, pair_recv_sem, cross_send_sem, cross_recv_sem, own_sem,
):
    me = lax.axis_index("ctx")
    fft = lax.axis_index("fft")
    chip = fft // 2
    core = fft % 2
    partner = chip * 2 + (1 - core)
    across = (1 - chip) * 2 + core
    tok_len, width = tok.shape
    block = w.shape[2]
    stretch = block // n_ctx
    rows = n_ctx * stretch
    n_taps = taps_in.shape[0]
    piece = tok_len // n_fft
    tc = min(128, tok_len)
    lc = min(128, block)
    per_lc = lc // stretch

    barrier = pltpu.get_barrier_semaphore()

    @pl.loop(1, n_ctx)
    def _(i):
        pl.semaphore_signal(barrier, inc=1, device_id={"ctx": lax.rem(me + i, n_ctx)}, device_id_type=MESH)

    for other in (partner, across):
        pl.semaphore_signal(barrier, inc=1, device_id={"fft": other}, device_id_type=MESH)

    loads = {}
    for slot, (name, src, dst) in enumerate([
        ("filt", filt_hbm, filt), ("tok", tok_hbm, tok), ("w1", w_hbm.at[1], w.at[1]), ("w2", w_hbm.at[2], w.at[2]),
        ("taps", taps_hbm, taps_in), ("gain", gain_hbm, gain_in), ("w0", w_hbm.at[0], w.at[0]),
        ("over", over_hbm, over), ("spread", spread_hbm, spread), ("turns", turns_hbm, turns),
        ("waves", waves_hbm, waves), ("wout", wout_hbm, wout),
    ]):
        loads[name] = pltpu.make_async_copy(src, dst, load_sem.at[slot])
        loads[name].start()

    loads["filt"].wait()
    flipped = filt[...].T
    for g in range(flipped.shape[0]):
        filt_send[g, 0, :] = flipped[g, :]

    pl.semaphore_wait(barrier, n_ctx - 1 + 2)

    first_group = fft * (block // group_size)

    def filt_copy(dest):
        return pltpu.make_async_remote_copy(
            src_ref=filt_send.at[first_group + (dest * stretch) // group_size],
            dst_ref=filt_recv.at[me],
            send_sem=filt_send_sem.at[dest], recv_sem=filt_recv_sem.at[me],
            device_id={"ctx": dest}, device_id_type=MESH,
        )

    def filt_arrival(src):
        return pltpu.make_async_remote_copy(
            src_ref=filt_send.at[0], dst_ref=filt_recv.at[src],
            send_sem=filt_send_sem.at[src], recv_sem=filt_recv_sem.at[src],
            device_id={"ctx": src}, device_id_type=MESH,
        )

    @pl.loop(1, n_ctx)
    def _(i):
        filt_copy(lax.rem(me + i, n_ctx)).start()

    own_filt = pltpu.make_async_copy(
        filt_send.at[first_group + (me * stretch) // group_size], filt_recv.at[me], own_sem.at[0])
    own_filt.start()

    def project(s):
        for n0 in range(0, block, min(256, block)):
            n1 = n0 + min(256, block)
            got = dot(tok[...], w[s, :, n0:n1])
            proj[s, RIM:, n0:n1] = got.astype(BF16).astype(F32)

    def rim_copy(s):
        return pltpu.make_async_remote_copy(
            src_ref=proj.at[s, pl.ds(tok_len, RIM), :], dst_ref=proj.at[s, pl.ds(0, RIM), :],
            send_sem=rim_send_sem.at[s], recv_sem=rim_recv_sem.at[s],
            device_id={"ctx": lax.rem(me + 1, n_ctx)}, device_id_type=MESH,
        )

    def send_rim(s):
        @pl.when(me < n_ctx - 1)
        def _():
            rim_copy(s).start()

        @pl.when(me == 0)
        def _():
            proj[s, 0:RIM, :] = jnp.zeros((RIM, block), F32)

    def finish_rim(s):
        @pl.when(me > 0)
        def _():
            rim_copy(s).wait_recv()

    loads["tok"].wait()
    for s, name in ((1, "w1"), (2, "w2")):
        loads[name].wait()
        project(s)
        send_rim(s)

    loads["taps"].wait()
    group_of = lax.broadcasted_iota(jnp.int32, (taps_in.shape[1], block), 1) // group_size
    group_at = lax.broadcasted_iota(jnp.int32, (taps_in.shape[1], block), 0)
    per_stream = taps_in.shape[1] // 3
    taps_of = []
    for s in range(3):
        pick = (group_at == group_of + (s * per_stream + first_group)).astype(F32)
        taps_of.append(dot(taps_in[...], pick, precision=lax.Precision.HIGHEST))

    def featurize(s, t0, c0):
        window = proj[s, pl.ds(t0, tc + RIM), c0:c0 + lc]
        total = None
        for j in range(n_taps):
            term = taps_of[s][j:j + 1, c0:c0 + lc] * window[RIM - j:RIM - j + tc, :]
            total = term if total is None else total + term
        return total.astype(BF16).astype(F32)

    def mix(t0, c0):
        both = featurize(1, t0, c0) * featurize(2, t0, c0)
        mixed[pl.ds(t0, tc), c0:c0 + lc] = both
        turned = both.T.reshape(per_lc, stretch, tc).astype(BF16)
        send[c0 // stretch:c0 // stretch + per_lc, :, pl.ds(t0, tc)] = turned

    for c0 in range(0, block, lc):
        @pl.loop(1, tok_len // tc)
        def _(t):
            mix(pl.multiple_of(t * tc, tc), c0)

    finish_rim(1)
    finish_rim(2)
    for c0 in range(0, block, lc):
        mix(0, c0)

    def swap(source, target, send_sem, recv_sem):
        def outgoing(dest):
            return pltpu.make_async_remote_copy(
                src_ref=source.at[dest], dst_ref=target.at[me],
                send_sem=send_sem.at[dest], recv_sem=recv_sem.at[me],
                device_id={"ctx": dest}, device_id_type=MESH,
            )

        def incoming(src):
            return pltpu.make_async_remote_copy(
                src_ref=source.at[src], dst_ref=target.at[src],
                send_sem=send_sem.at[src], recv_sem=recv_sem.at[src],
                device_id={"ctx": src}, device_id_type=MESH,
            )

        return outgoing, incoming

    go_out, go_in = swap(send, recv, go_send_sem, go_recv_sem)

    @pl.loop(1, n_ctx)
    def _(i):
        go_out(lax.rem(me + i, n_ctx)).start()

    own_go = pltpu.make_async_copy(send.at[me], recv.at[me], own_sem.at[1])
    own_go.start()

    loads["w0"].wait()
    project(0)
    send_rim(0)
    loads["spread"].wait()
    spread_t[...] = spread[...].T

    loads["over"].wait()
    loads["turns"].wait()
    loads["waves"].wait()
    own_filt.wait()

    @pl.loop(1, n_ctx)
    def _(i):
        filt_arrival(lax.rem(me + i, n_ctx)).wait_recv()

    lags = filt_recv[:, 0, :].astype(BF16)
    first = dot(over[...].astype(BF16), lags)
    f_re, f_im = first[:n_ctx], first[n_ctx:]
    t_re, t_im = turns[0], turns[1]
    g_re = (f_re * t_re - f_im * t_im).astype(BF16)
    g_im = (f_re * t_im + f_im * t_re).astype(BF16)
    top = jnp.concatenate([g_re, g_im], axis=1)
    bottom = jnp.concatenate([g_im, -g_re], axis=1)
    scale = 1.0 / (n_ctx * tok_len)
    spec[0] = dot(top, waves[...]) * scale
    spec[1] = dot(bottom, waves[...]) * scale

    finish_rim(0)
    loads["gain"].wait()

    for c0 in range(0, block, lc):
        @pl.loop(0, tok_len // tc)
        def _(t):
            t0 = pl.multiple_of(t * tc, tc)
            query[pl.ds(t0, tc), c0:c0 + lc] = featurize(0, t0, c0)

    own_go.wait()

    @pl.loop(1, n_ctx)
    def _(i):
        go_in(lax.rem(me + i, n_ctx)).wait_recv()

    kc = min(8, n_ctx)
    kr = kc * stretch

    @pl.loop(0, n_ctx // kc)
    def _(i):
        got = recv[pl.ds(i * kc, kc)].astype(F32)
        signal[pl.ds(pl.multiple_of(i * kr, kr), kr), :] = got.reshape(kr, tok_len).astype(BF16)

    mc = min(256, rows)
    lt = min(128, tok_len)

    for m0 in range(0, 2 * rows, mc):
        stage[m0:m0 + mc, :] = dot(spread[m0:m0 + mc, :], signal[...])

    def pieces(i, n0, table):
        k0 = pl.multiple_of(i * kr, kr)
        re = stage[pl.ds(k0, kr), n0:n0 + lt].reshape(kc, stretch, lt)
        im = stage[pl.ds(rows + k0, kr), n0:n0 + lt].reshape(kc, stretch, lt)
        b_re = table[0, pl.ds(pl.multiple_of(i * kc, kc), kc), n0:n0 + lt][:, None, :]
        b_im = table[1, pl.ds(pl.multiple_of(i * kc, kc), kc), n0:n0 + lt][:, None, :]
        return k0, re, im, b_re, b_im

    @pl.loop(0, n_ctx // kc)
    def _(i):
        for n0 in range(0, tok_len, lt):
            k0, re, im, b_re, b_im = pieces(i, n0, turns)
            o_re = (re * b_re - im * b_im).reshape(kr, lt)
            o_im = (re * b_im + im * b_re).reshape(kr, lt)
            lhs[pl.ds(k0, kr), n0:n0 + lt] = o_re.astype(BF16)
            lhs[pl.ds(k0, kr), tok_len + n0:tok_len + n0 + lt] = o_im.astype(BF16)
            lhs[pl.ds(rows + k0, kr), n0:n0 + lt] = o_im.astype(BF16)
            lhs[pl.ds(rows + k0, kr), tok_len + n0:tok_len + n0 + lt] = (-o_re).astype(BF16)

    for m0 in range(0, 2 * rows, mc):
        stage[m0:m0 + mc, :] = dot(lhs[m0:m0 + mc, :], waves[...])

    @pl.loop(0, n_ctx // kc)
    def _(i):
        for n0 in range(0, tok_len, lt):
            k0, re, im, b_re, b_im = pieces(i, n0, spec)
            o_re = (re * b_re - im * b_im).reshape(kr, lt)
            o_im = (re * b_im + im * b_re).reshape(kr, lt)
            lhs[pl.ds(k0, kr), n0:n0 + lt] = o_re.astype(BF16)
            lhs[pl.ds(k0, kr), tok_len + n0:tok_len + n0 + lt] = (-o_im).astype(BF16)
            lhs[pl.ds(rows + k0, kr), n0:n0 + lt] = o_im.astype(BF16)
            lhs[pl.ds(rows + k0, kr), tok_len + n0:tok_len + n0 + lt] = o_re.astype(BF16)

    for m0 in range(0, 2 * rows, mc):
        stage[m0:m0 + mc, :] = dot(lhs[m0:m0 + mc, :], waves[...])

    @pl.loop(0, n_ctx // kc)
    def _(i):
        for n0 in range(0, tok_len, lt):
            k0, re, im, b_re, b_im = pieces(i, n0, turns)
            o_re = (re * b_re + im * b_im).reshape(kr, lt)
            o_im = (im * b_re - re * b_im).reshape(kr, lt)
            back[pl.ds(k0, kr), n0:n0 + lt] = o_re.astype(BF16)
            back[pl.ds(rows + k0, kr), n0:n0 + lt] = o_im.astype(BF16)

    for m0 in range(0, rows, mc):
        got = dot(spread_t[m0:m0 + mc, :], back[...])
        send2[m0 // stretch:(m0 + mc) // stretch] = got.reshape(mc // stretch, stretch, tok_len).astype(BF16)

    come_out, come_in = swap(send2, recv2, come_send_sem, come_recv_sem)

    @pl.loop(1, n_ctx)
    def _(i):
        come_out(lax.rem(me + i, n_ctx)).start()

    own_come = pltpu.make_async_copy(send2.at[me], recv2.at[me], own_sem.at[2])
    own_come.start()

    loads["wout"].wait()
    own_come.wait()

    @pl.loop(1, n_ctx)
    def _(i):
        come_in(lax.rem(me + i, n_ctx)).wait_recv()

    gain_row = gain_in[:, pl.ds(pl.multiple_of(fft * block, block), block)]
    for c0 in range(0, block, lc):
        @pl.loop(0, tok_len // tc)
        def _(t):
            t0 = pl.multiple_of(t * tc, tc)
            got = recv2[c0 // stretch:c0 // stretch + per_lc, :, pl.ds(t0, tc)].astype(F32)
            conv = got.reshape(lc, tc).T
            whole = conv + gain_row[:, c0:c0 + lc] * mixed[pl.ds(t0, tc), c0:c0 + lc]
            gated[pl.ds(t0, tc), c0:c0 + lc] = (query[pl.ds(t0, tc), c0:c0 + lc] * whole).astype(BF16)

    oc = min(512, width)

    def partial(owner, n0):
        return dot(gated[pl.ds(pl.multiple_of(owner * piece, piece), piece), :], wout[:, n0:n0 + oc])

    def pair_copy(i):
        return pltpu.make_async_remote_copy(
            src_ref=pair_send.at[i], dst_ref=pair_recv.at[i],
            send_sem=pair_send_sem.at[i], recv_sem=pair_recv_sem.at[i],
            device_id={"fft": partner}, device_id_type=MESH,
        )

    cross_copy = pltpu.make_async_remote_copy(
        src_ref=cross_send, dst_ref=cross_recv, send_sem=cross_send_sem, recv_sem=cross_recv_sem,
        device_id={"fft": across}, device_id_type=MESH,
    )

    for i, owner in ((0, (1 - chip) * 2 + (1 - core)), (1, partner)):
        for n0 in range(0, width, oc):
            pair_send[i, :, n0:n0 + oc] = partial(owner, n0).astype(BF16)
        pair_copy(i).start()

    for n0 in range(0, width, oc):
        kept[:, n0:n0 + oc] = partial(across, n0)
    pair_copy(0).wait_recv()
    for n0 in range(0, width, oc):
        cross_send[:, n0:n0 + oc] = (kept[:, n0:n0 + oc] + pair_recv[0, :, n0:n0 + oc].astype(F32)).astype(BF16)
    cross_copy.start()
    for n0 in range(0, width, oc):
        kept[:, n0:n0 + oc] = partial(fft, n0)
    pair_copy(1).wait_recv()
    for n0 in range(0, width, oc):
        kept[:, n0:n0 + oc] = kept[:, n0:n0 + oc] + pair_recv[1, :, n0:n0 + oc].astype(F32)
    cross_copy.wait_recv()
    for n0 in range(0, width, oc):
        out_ref[:, n0:n0 + oc] = (kept[:, n0:n0 + oc] + cross_recv[:, n0:n0 + oc].astype(F32)).astype(BF16)

    pair_copy(0).wait_send()
    pair_copy(1).wait_send()
    cross_copy.wait_send()

    @pl.when(me < n_ctx - 1)
    def _():
        for s in range(3):
            rim_copy(s).wait_send()

    @pl.loop(1, n_ctx)
    def _(i):
        dest = lax.rem(me + i, n_ctx)
        filt_copy(dest).wait_send()
        go_out(dest).wait_send()
        come_out(dest).wait_send()


def body(tokens, w_in, short_taps, long_filter, skip_gain, w_out):
    n_ctx = lax.axis_size("ctx")
    n_fft = lax.axis_size("fft")
    tok_len, width = tokens.shape
    block = w_in.shape[2]
    n_groups = long_filter.shape[1]
    group_size = width // n_groups
    stretch = block // n_ctx
    rows = n_ctx * stretch
    piece = tok_len // n_fft
    over, spread, turns, waves = tables(n_ctx, tok_len, stretch)
    dma = pltpu.SemaphoreType.DMA
    vmem = pltpu.VMEM
    streams = w_in.transpose(1, 0, 2)
    args = (
        tokens, streams, short_taps, long_filter, skip_gain.reshape(1, width), w_out,
        jnp.asarray(over), jnp.asarray(spread), jnp.asarray(turns), jnp.asarray(waves),
    )
    return pl.pallas_call(
        functools.partial(kernel, n_ctx, n_fft, group_size),
        out_shape=jax.ShapeDtypeStruct((piece, width), BF16),
        in_specs=[pl.BlockSpec(memory_space=pl.ANY)] * len(args),
        out_specs=pl.BlockSpec(memory_space=vmem),
        scratch_shapes=[vmem(a.shape, a.dtype) for a in args] + [
            vmem((rows, 2 * rows), BF16),
            vmem((3, tok_len + RIM, block), F32),
            vmem((tok_len, block), F32),
            vmem((tok_len, block), F32),
            vmem((n_ctx, stretch, tok_len), BF16),
            vmem((n_ctx, stretch, tok_len), BF16),
            vmem((n_groups, 1, tok_len), F32),
            vmem((n_ctx, 1, tok_len), F32),
            vmem((rows, tok_len), BF16),
            vmem((2 * rows, tok_len), F32),
            vmem((2 * rows, 2 * tok_len), BF16),
            vmem((2, n_ctx, tok_len), F32),
            vmem((2 * rows, tok_len), BF16),
            vmem((n_ctx, stretch, tok_len), BF16),
            vmem((n_ctx, stretch, tok_len), BF16),
            vmem((tok_len, block), BF16),
            vmem((piece, width), F32),
            vmem((2, piece, width), BF16),
            vmem((2, piece, width), BF16),
            vmem((piece, width), BF16),
            vmem((piece, width), BF16),
            dma((12,)), dma((3,)), dma((3,)),
            dma((n_ctx,)), dma((n_ctx,)), dma((n_ctx,)), dma((n_ctx,)), dma((n_ctx,)), dma((n_ctx,)),
            dma((2,)), dma((2,)), dma, dma, dma((3,)),
        ],
        compiler_params=pltpu.CompilerParams(
            collective_id=0, has_side_effects=True, vmem_limit_bytes=60 * 1024 * 1024
        ),
        name="hyena",
    )(*args)


def solution(mesh):
    return jax.shard_map(
        body,
        mesh=mesh,
        in_specs=(P("ctx", None), P(None, None, "fft"), P(), P("ctx", None), P(), P("fft", None)),
        out_specs=P(("ctx", "fft"), None),
        check_vma=False,
    )
```

```python
import functools
import math

import jax
import jax.numpy as jnp
import numpy as np
from jax import lax
from jax.experimental import pallas as pl
from jax.experimental.pallas import tpu as pltpu
from jax.sharding import PartitionSpec as P

MESH = pl.DeviceIdType.MESH
F32 = jnp.float32
BF16 = jnp.bfloat16
RIM = 8


def tables(n_ctx, tok_len, stretch):
    blocks = np.arange(n_ctx)
    lags = np.arange(tok_len)
    odd = 2 * blocks + 1
    angle = (odd[:, None] * blocks[None, :] % (4 * n_ctx)) * (2.0 * math.pi / (4 * n_ctx))
    eye = np.eye(stretch)
    over_blocks = np.concatenate([np.cos(angle), -np.sin(angle)], axis=0)
    spread = np.kron(over_blocks, eye)
    turn = (odd[:, None] * lags[None, :]) * (2.0 * math.pi / (4 * n_ctx * tok_len))
    turns = np.stack([np.cos(turn), -np.sin(turn)])
    inner = (lags[:, None] * lags[None, :] % tok_len) * (2.0 * math.pi / tok_len)
    waves = np.concatenate([np.cos(inner), np.sin(inner)], axis=0)
    return (
        over_blocks.astype(np.float32),
        spread.astype(np.float32).astype(jnp.bfloat16),
        turns.astype(np.float32),
        waves.astype(np.float32).astype(jnp.bfloat16),
    )


def dot(a, b, **kw):
    return jnp.dot(a, b, preferred_element_type=F32, **kw)


def kernel(
    n_ctx, n_fft, group_size,
    tok_hbm, w_hbm, taps_hbm, filt_hbm, gain_hbm, wout_hbm, over_hbm, spread_hbm, turns_hbm, waves_hbm,
    out_ref,
    tok, w, taps_in, filt, gain_in, wout, over, spread, turns, waves,
    spread_t, proj, mixed, query, send, recv, filt_send, filt_recv,
    signal, stage, lhs, spec, back, send2, recv2, gated, part, kept,
    pair_send, pair_recv, cross_send, cross_recv,
    load_sem, rim_send_sem, rim_recv_sem, filt_sem, go_send_sem, go_recv_sem, come_send_sem, come_recv_sem,
    pair_send_sem, pair_recv_sem, cross_send_sem, cross_recv_sem,
):
    me = lax.axis_index("ctx")
    fft = lax.axis_index("fft")
    chip = fft // 2
    core = fft % 2
    partner = chip * 2 + (1 - core)
    across = (1 - chip) * 2 + core
    tok_len, width = tok.shape
    block = w.shape[2]
    stretch = block // n_ctx
    rows = n_ctx * stretch
    n_taps = taps_in.shape[0]
    piece = tok_len // n_fft
    half = tok_len // 2
    tc = min(128, half)
    lc = min(128, block)
    per_lc = lc // stretch

    barrier = pltpu.get_barrier_semaphore()

    def each_peer(act):
        @pl.loop(1, n_ctx)
        def _(i):
            m = n_ctx - i
            d = (m + 1) // 2
            odd = m % 2
            act(lax.rem(me + odd * d + (1 - odd) * (n_ctx - d), n_ctx))

    each_peer(lambda peer: pl.semaphore_signal(barrier, inc=1, device_id={"ctx": peer}, device_id_type=MESH))
    for other in (partner, across):
        pl.semaphore_signal(barrier, inc=1, device_id={"fft": other}, device_id_type=MESH)

    split = half - 16
    loads = {}
    for slot, (name, src, dst) in enumerate([
        ("taps", taps_hbm, taps_in),
        ("tok1", tok_hbm.at[pl.ds(split, tok_len - split)], tok.at[pl.ds(split, tok_len - split)]),
        ("w1", w_hbm.at[1], w.at[1]), ("w2", w_hbm.at[2], w.at[2]),
        ("tok0", tok_hbm.at[pl.ds(0, split)], tok.at[pl.ds(0, split)]),
        ("filt", filt_hbm, filt), ("w0", w_hbm.at[0], w.at[0]), ("gain", gain_hbm, gain_in),
        ("spread", spread_hbm, spread), ("over", over_hbm, over), ("turns", turns_hbm, turns),
        ("waves", waves_hbm, waves), ("wout", wout_hbm, wout),
    ]):
        loads[name] = pltpu.make_async_copy(src, dst, load_sem.at[slot])
        loads[name].start()

    first_group = fft * (block // group_size)
    per_stream = taps_in.shape[1] // 3
    loads["taps"].wait()
    group_of = lax.broadcasted_iota(jnp.int32, (per_stream, block), 1) // group_size + first_group
    pick = (lax.broadcasted_iota(jnp.int32, (per_stream, block), 0) == group_of).astype(F32)
    blank = jnp.zeros((8 - n_taps, per_stream), F32)
    taps_rows = jnp.concatenate(
        [x for s in range(3) for x in (taps_in[:, s * per_stream:(s + 1) * per_stream], blank)], axis=0
    )
    taps_all = dot(taps_rows, pick, precision=lax.Precision.HIGHEST)

    def project(s, r0, r1):
        for n0 in range(0, block, min(256, block)):
            n1 = n0 + min(256, block)
            got = dot(tok[r0:r1, :], w[s, :, n0:n1])
            proj[s, RIM + r0:RIM + r1, n0:n1] = got.astype(BF16).astype(F32)

    def rim_copy(s):
        return pltpu.make_async_remote_copy(
            src_ref=proj.at[s, pl.ds(tok_len, RIM), :], dst_ref=proj.at[s, pl.ds(0, RIM), :],
            send_sem=rim_send_sem.at[s], recv_sem=rim_recv_sem.at[s],
            device_id={"ctx": lax.rem(me + 1, n_ctx)}, device_id_type=MESH,
        )

    def send_rim(s):
        @pl.when(me < n_ctx - 1)
        def _():
            rim_copy(s).start()

        @pl.when(me == 0)
        def _():
            proj[s, 0:RIM, :] = jnp.zeros((RIM, block), F32)

    def finish_rim(s):
        @pl.when(me > 0)
        def _():
            rim_copy(s).wait_recv()

    def featurize(s, t0, c0):
        window = proj[s, pl.ds(t0, tc + RIM), c0:c0 + lc]
        total = None
        for j in range(n_taps):
            term = taps_all[s * 8 + j:s * 8 + j + 1, c0:c0 + lc] * window[RIM - j:RIM - j + tc, :]
            total = term if total is None else total + term
        return total.astype(BF16).astype(F32)

    def mix(t0, c0):
        both = featurize(1, t0, c0) * featurize(2, t0, c0)
        mixed[pl.ds(t0, tc), c0:c0 + lc] = both
        turned = both.T.reshape(per_lc, stretch, tc).astype(BF16)
        send[c0 // stretch:c0 // stretch + per_lc, :, pl.ds(t0, tc)] = turned

    def exchange(source, target, send_sem, recv_sem):
        def at(ref, where, h0):
            return ref.at[where, :, pl.ds(h0, half)]

        def copy_to(dest, h0, i):
            return pltpu.make_async_remote_copy(
                src_ref=at(source, dest, h0), dst_ref=at(target, me, h0),
                send_sem=send_sem.at[i], recv_sem=recv_sem.at[i],
                device_id={"ctx": dest}, device_id_type=MESH,
            )

        def start(h0, i):
            each_peer(lambda dest: copy_to(dest, h0, i).start())
            target[me, :, pl.ds(h0, half)] = source[me, :, pl.ds(h0, half)]

        def all_of(h0, i):
            return pltpu.make_async_remote_copy(
                src_ref=at(source, pl.ds(0, n_ctx - 1), h0), dst_ref=at(target, pl.ds(0, n_ctx - 1), h0),
                send_sem=send_sem.at[i], recv_sem=recv_sem.at[i],
                device_id={"ctx": lax.rem(me + 1, n_ctx)}, device_id_type=MESH,
            )

        return start, all_of

    go_start, go_all = exchange(send, recv, go_send_sem, go_recv_sem)

    loads["tok1"].wait()
    for s, name in ((1, "w1"), (2, "w2")):
        loads[name].wait()
        project(s, split, tok_len)
    for c0 in range(0, block, lc):
        @pl.loop(half // tc, tok_len // tc)
        def _(t):
            mix(pl.multiple_of(t * tc, tc), c0)

    pl.semaphore_wait(barrier, n_ctx - 1 + 2)
    send_rim(1)
    send_rim(2)
    go_start(half, 1)

    loads["tok0"].wait()
    project(1, 0, split)
    project(2, 0, split)
    for c0 in range(0, block, lc):
        @pl.loop(1, half // tc)
        def _(t):
            mix(pl.multiple_of(t * tc, tc), c0)

    finish_rim(1)
    finish_rim(2)
    for c0 in range(0, block, lc):
        mix(0, c0)
    go_start(0, 0)

    loads["filt"].wait()
    flipped = filt[...].T.astype(BF16).astype(F32)
    lag_rows, lag_lanes = filt_send.shape[1:]
    for j in range(lag_rows):
        filt_send[:, j, :] = flipped[:, j * lag_lanes:(j + 1) * lag_lanes].astype(BF16)

    def filt_copy(dest):
        return pltpu.make_async_remote_copy(
            src_ref=filt_send.at[first_group + (dest * stretch) // group_size],
            dst_ref=filt_recv.at[me],
            send_sem=filt_sem.at[0], recv_sem=filt_sem.at[1],
            device_id={"ctx": dest}, device_id_type=MESH,
        )

    filt_all = pltpu.make_async_remote_copy(
        src_ref=filt_recv.at[pl.ds(0, n_ctx - 1)], dst_ref=filt_recv.at[pl.ds(0, n_ctx - 1)],
        send_sem=filt_sem.at[0], recv_sem=filt_sem.at[1],
        device_id={"ctx": lax.rem(me + 1, n_ctx)}, device_id_type=MESH,
    )
    each_peer(lambda dest: filt_copy(dest).start())
    filt_recv[me] = filt_send[first_group + (me * stretch) // group_size]

    loads["w0"].wait()
    project(0, 0, tok_len)
    send_rim(0)
    loads["spread"].wait()
    spread_t[...] = spread[...].T
    finish_rim(0)
    for c0 in range(0, block, lc):
        @pl.loop(0, tok_len // tc)
        def _(t):
            t0 = pl.multiple_of(t * tc, tc)
            query[pl.ds(t0, tc), c0:c0 + lc] = featurize(0, t0, c0)

    kc = min(8, n_ctx)
    kr = kc * stretch
    mc = min(256, rows)
    lt = min(128, half)

    def pieces(i, n0, table):
        k0 = pl.multiple_of(i * kr, kr)
        cols = pl.ds(n0, lt)
        re = stage[pl.ds(k0, kr), cols].reshape(kc, stretch, lt)
        im = stage[pl.ds(rows + k0, kr), cols].reshape(kc, stretch, lt)
        b_re = table[0, pl.ds(pl.multiple_of(i * kc, kc), kc), cols][:, None, :]
        b_im = table[1, pl.ds(pl.multiple_of(i * kc, kc), kc), cols][:, None, :]
        return k0, re, im, b_re, b_im

    loads["turns"].wait()

    def first_stage(h0):
        @pl.loop(0, n_ctx // kc)
        def _(i):
            got = recv[pl.ds(i * kc, kc), :, h0:h0 + half].astype(F32)
            signal[pl.ds(pl.multiple_of(i * kr, kr), kr), h0:h0 + half] = got.reshape(kr, half).astype(BF16)

        for m0 in range(0, 2 * rows, mc):
            stage[m0:m0 + mc, h0:h0 + half] = dot(spread[m0:m0 + mc, :], signal[:, h0:h0 + half])

        @pl.loop(0, n_ctx // kc)
        def _(i):
            for n0 in range(h0, h0 + half, lt):
                k0, re, im, b_re, b_im = pieces(i, n0, turns)
                o_re = (re * b_re - im * b_im).reshape(kr, lt)
                o_im = (re * b_im + im * b_re).reshape(kr, lt)
                lhs[pl.ds(k0, kr), n0:n0 + lt] = o_re.astype(BF16)
                lhs[pl.ds(k0, kr), tok_len + n0:tok_len + n0 + lt] = o_im.astype(BF16)
                lhs[pl.ds(rows + k0, kr), n0:n0 + lt] = o_im.astype(BF16)
                lhs[pl.ds(rows + k0, kr), tok_len + n0:tok_len + n0 + lt] = (-o_re).astype(BF16)

    go_all(half, 1).wait_recv()
    first_stage(half)

    loads["over"].wait()
    loads["waves"].wait()
    filt_all.wait_recv()
    lags3 = filt_recv[...].astype(F32)
    lags = jnp.concatenate([lags3[:, j, :] for j in range(lag_rows)], axis=1).astype(BF16)
    first = dot(over[...].astype(BF16), lags)
    f_re, f_im = first[:n_ctx], first[n_ctx:]
    t_re, t_im = turns[0], turns[1]
    g_re = (f_re * t_re - f_im * t_im).astype(BF16)
    g_im = (f_re * t_im + f_im * t_re).astype(BF16)
    top = jnp.concatenate([g_re, g_im], axis=1)
    bottom = jnp.concatenate([g_im, -g_re], axis=1)
    scale = 1.0 / (n_ctx * tok_len)
    spec[0] = dot(top, waves[...]) * scale
    spec[1] = dot(bottom, waves[...]) * scale

    go_all(0, 0).wait_recv()
    first_stage(0)

    for m0 in range(0, 2 * rows, mc):
        stage[m0:m0 + mc, :] = dot(lhs[m0:m0 + mc, :], waves[...])

    @pl.loop(0, n_ctx // kc)
    def _(i):
        for n0 in range(0, tok_len, lt):
            k0, re, im, b_re, b_im = pieces(i, n0, spec)
            o_re = (re * b_re - im * b_im).reshape(kr, lt)
            o_im = (re * b_im + im * b_re).reshape(kr, lt)
            lhs[pl.ds(k0, kr), n0:n0 + lt] = o_re.astype(BF16)
            lhs[pl.ds(k0, kr), tok_len + n0:tok_len + n0 + lt] = (-o_im).astype(BF16)
            lhs[pl.ds(rows + k0, kr), n0:n0 + lt] = o_im.astype(BF16)
            lhs[pl.ds(rows + k0, kr), tok_len + n0:tok_len + n0 + lt] = o_re.astype(BF16)

    come_start, come_all = exchange(send2, recv2, come_send_sem, come_recv_sem)

    def last_stage(h0, i):
        for m0 in range(0, 2 * rows, mc):
            stage[m0:m0 + mc, pl.ds(h0, half)] = dot(lhs[m0:m0 + mc, :], waves[:, pl.ds(h0, half)])

        @pl.loop(0, n_ctx // kc)
        def _(i):
            for j in range(half // lt):
                n0 = pl.multiple_of(h0 + j * lt, lt)
                k0, re, im, b_re, b_im = pieces(i, n0, turns)
                o_re = (re * b_re + im * b_im).reshape(kr, lt)
                o_im = (im * b_re - re * b_im).reshape(kr, lt)
                back[pl.ds(k0, kr), pl.ds(n0, lt)] = o_re.astype(BF16)
                back[pl.ds(rows + k0, kr), pl.ds(n0, lt)] = o_im.astype(BF16)

        for m0 in range(0, rows, mc):
            got = dot(spread_t[m0:m0 + mc, :], back[:, pl.ds(h0, half)])
            send2[m0 // stretch:(m0 + mc) // stretch, :, pl.ds(h0, half)] = (
                got.reshape(mc // stretch, stretch, half).astype(BF16))
        come_start(h0, i)

    theirs = pl.multiple_of((1 - chip) * half, half)
    ours = pl.multiple_of(chip * half, half)
    last_stage(theirs, 0)
    last_stage(ours, 1)

    loads["wout"].wait()
    loads["gain"].wait()
    gain_row = gain_in[:, pl.ds(pl.multiple_of(fft * block, block), block)]
    n_chunks, oc = pair_send.shape[1], pair_send.shape[3]

    def gate(h0):
        for c0 in range(0, block, lc):
            @pl.loop(0, half // tc)
            def _(t):
                t0 = pl.multiple_of(h0 + t * tc, tc)
                got = recv2[c0 // stretch:c0 // stretch + per_lc, :, pl.ds(t0, tc)].astype(F32)
                conv = got.reshape(lc, tc).T
                whole = conv + gain_row[:, c0:c0 + lc] * mixed[pl.ds(t0, tc), c0:c0 + lc]
                gated[pl.ds(t0, tc), c0:c0 + lc] = (query[pl.ds(t0, tc), c0:c0 + lc] * whole).astype(BF16)

    def pair_copy(i, n):
        return pltpu.make_async_remote_copy(
            src_ref=pair_send.at[i, n], dst_ref=pair_recv.at[i, n],
            send_sem=pair_send_sem.at[i, n], recv_sem=pair_recv_sem.at[i, n],
            device_id={"fft": partner}, device_id_type=MESH,
        )

    def cross_copy(n):
        return pltpu.make_async_remote_copy(
            src_ref=cross_send.at[n], dst_ref=cross_recv.at[n],
            send_sem=cross_send_sem.at[n], recv_sem=cross_recv_sem.at[n],
            device_id={"fft": across}, device_id_type=MESH,
        )

    def partials(h0, i):
        for n in range(n_chunks):
            part[n] = dot(gated[pl.ds(h0, half), :], wout[:, n * oc:(n + 1) * oc])
            pair_send[i, n] = part[n, pl.ds(pl.multiple_of((1 - core) * piece, piece), piece), :].astype(BF16)
            pair_copy(i, n).start()

    def pair_sum(i, n):
        pair_copy(i, n).wait_recv()
        return part[n, pl.ds(pl.multiple_of(core * piece, piece), piece), :] + pair_recv[i, n].astype(F32)

    go_all(half, 1).wait_send()
    go_all(0, 0).wait_send()
    filt_all.wait_send()

    @pl.when(me < n_ctx - 1)
    def _():
        for s in range(3):
            rim_copy(s).wait_send()

    come_all(theirs, 0).wait_recv()
    gate(theirs)
    partials(theirs, 0)
    for n in range(n_chunks):
        cross_send[n] = pair_sum(0, n).astype(BF16)
        cross_copy(n).start()

    come_all(ours, 1).wait_recv()
    gate(ours)
    partials(ours, 1)
    for n in range(n_chunks):
        kept[n] = pair_sum(1, n)

    come_all(theirs, 0).wait_send()
    come_all(ours, 1).wait_send()
    for n in range(n_chunks):
        pair_copy(0, n).wait_send()
        pair_copy(1, n).wait_send()
    for n in range(n_chunks):
        cross_copy(n).wait_recv()
        out_ref[:, n * oc:(n + 1) * oc] = (kept[n] + cross_recv[n].astype(F32)).astype(BF16)
    for n in range(n_chunks):
        cross_copy(n).wait_send()


def body(tokens, w_in, short_taps, long_filter, skip_gain, w_out):
    n_ctx = lax.axis_size("ctx")
    n_fft = lax.axis_size("fft")
    tok_len, width = tokens.shape
    block = w_in.shape[2]
    n_groups = long_filter.shape[1]
    group_size = width // n_groups
    stretch = block // n_ctx
    rows = n_ctx * stretch
    piece = tok_len // n_fft
    oc = min(512, width)
    n_chunks = width // oc
    lag_rows = 4
    over, spread, turns, waves = tables(n_ctx, tok_len, stretch)
    dma = pltpu.SemaphoreType.DMA
    vmem = pltpu.VMEM
    streams = w_in.transpose(1, 0, 2)
    args = (
        tokens, streams, short_taps, long_filter, skip_gain.reshape(1, width), w_out,
        jnp.asarray(over), jnp.asarray(spread), jnp.asarray(turns), jnp.asarray(waves),
    )
    return pl.pallas_call(
        functools.partial(kernel, n_ctx, n_fft, group_size),
        out_shape=jax.ShapeDtypeStruct((piece, width), BF16),
        in_specs=[pl.BlockSpec(memory_space=pl.ANY)] * len(args),
        out_specs=pl.BlockSpec(memory_space=vmem),
        scratch_shapes=[vmem(a.shape, a.dtype) for a in args] + [
            vmem((rows, 2 * rows), BF16),
            vmem((3, tok_len + RIM, block), F32),
            vmem((tok_len, block), F32),
            vmem((tok_len, block), F32),
            vmem((n_ctx, stretch, tok_len), BF16),
            vmem((n_ctx, stretch, tok_len), BF16),
            vmem((n_groups, lag_rows, tok_len // lag_rows), BF16),
            vmem((n_ctx, lag_rows, tok_len // lag_rows), BF16),
            vmem((rows, tok_len), BF16),
            vmem((2 * rows, tok_len), F32),
            vmem((2 * rows, 2 * tok_len), BF16),
            vmem((2, n_ctx, tok_len), F32),
            vmem((2 * rows, tok_len), BF16),
            vmem((n_ctx, stretch, tok_len), BF16),
            vmem((n_ctx, stretch, tok_len), BF16),
            vmem((tok_len, block), BF16),
            vmem((n_chunks, tok_len // 2, oc), F32),
            vmem((n_chunks, piece, oc), F32),
            vmem((2, n_chunks, piece, oc), BF16),
            vmem((2, n_chunks, piece, oc), BF16),
            vmem((n_chunks, piece, oc), BF16),
            vmem((n_chunks, piece, oc), BF16),
            dma((13,)), dma((3,)), dma((3,)), dma((2,)), dma((2,)), dma((2,)), dma((2,)), dma((2,)),
            dma((2, n_chunks)), dma((2, n_chunks)), dma((n_chunks,)), dma((n_chunks,)),
        ],
        compiler_params=pltpu.CompilerParams(
            collective_id=0, has_side_effects=True, vmem_limit_bytes=60 * 1024 * 1024
        ),
        name="hyena",
    )(*args)


def solution(mesh):
    return jax.shard_map(
        body,
        mesh=mesh,
        in_specs=(P("ctx", None), P(None, None, "fft"), P(), P("ctx", None), P(), P("fft", None)),
        out_specs=P(("ctx", "fft"), None),
        check_vma=False,
    )
```

```python
import functools
import math

import jax
import jax.numpy as jnp
import numpy as np
from jax import lax
from jax.experimental import pallas as pl
from jax.experimental.pallas import tpu as pltpu
from jax.sharding import PartitionSpec as P

MESH = pl.DeviceIdType.MESH
F32 = jnp.float32
BF16 = jnp.bfloat16
RIM = 8


def tables(n_ctx, tok_len, stretch):
    blocks = np.arange(n_ctx)
    lags = np.arange(tok_len)
    odd = 2 * blocks + 1
    angle = (odd[:, None] * blocks[None, :] % (4 * n_ctx)) * (2.0 * math.pi / (4 * n_ctx))
    eye = np.eye(stretch)
    over_blocks = np.concatenate([np.cos(angle), -np.sin(angle)], axis=0)
    spread = np.kron(over_blocks, eye)
    turn = (odd[:, None] * lags[None, :]) * (2.0 * math.pi / (4 * n_ctx * tok_len))
    turns = np.stack([np.cos(turn), -np.sin(turn)])
    inner = (lags[:, None] * lags[None, :] % tok_len) * (2.0 * math.pi / tok_len)
    waves = np.concatenate([np.cos(inner), np.sin(inner)], axis=0)
    return (
        over_blocks.astype(np.float32),
        spread.astype(np.float32).astype(jnp.bfloat16),
        turns.astype(np.float32),
        waves.astype(np.float32).astype(jnp.bfloat16),
    )


def dot(a, b, **kw):
    return jnp.dot(a, b, preferred_element_type=F32, **kw)


def kernel(
    n_ctx, n_fft, group_size,
    tok_hbm, w_hbm, taps_hbm, filt_hbm, gain_hbm, wout_hbm, over_hbm, spread_hbm, turns_hbm, waves_hbm,
    kept_out, cross_out,
    tok, w, taps_in, filt, gain_in, wout, over, spread, turns, waves,
    spread_t, proj, mixed, query, send, recv, filt_send, filt_recv,
    signal, lhs, lhs2, spec, back, send2, recv2, gated, part, kept,
    pair_send, pair_recv, cross_send,
    load_sem, rim_send_sem, rim_recv_sem, filt_sem, go_send_sem, go_recv_sem, come_send_sem, come_recv_sem,
    pair_send_sem, pair_recv_sem, cross_send_sem, cross_recv_sem,
):
    me = lax.axis_index("ctx")
    fft = lax.axis_index("fft")
    chip = fft // 2
    core = fft % 2
    partner = chip * 2 + (1 - core)
    across = (1 - chip) * 2 + core
    tok_len, width = tok.shape
    block = w.shape[2]
    stretch = block // n_ctx
    rows = n_ctx * stretch
    n_taps = taps_in.shape[0]
    piece = tok_len // n_fft
    half = tok_len // 2
    tc = min(128, half)
    lc = min(128, block)
    per_lc = lc // stretch

    barrier = pltpu.get_barrier_semaphore()

    def each_peer(act):
        group = next(g for g in (9, 7, 5, 3, 1) if (n_ctx - 1) % g == 0)

        @pl.loop(0, (n_ctx - 1) // group)
        def _(i):
            for j in range(group):
                m = n_ctx - 1 - j - i * group
                d = (m + 1) // 2
                odd = m % 2
                act(lax.rem(me + odd * d + (1 - odd) * (n_ctx - d), n_ctx))

    split = half - 16
    loads = {}
    for slot, (name, src, dst) in enumerate([
        ("taps", taps_hbm, taps_in),
        ("tok1", tok_hbm.at[pl.ds(split, tok_len - split)], tok.at[pl.ds(split, tok_len - split)]),
        ("w1", w_hbm.at[1], w.at[1]), ("w2", w_hbm.at[2], w.at[2]),
        ("filt", filt_hbm, filt), ("tok0", tok_hbm.at[pl.ds(0, split)], tok.at[pl.ds(0, split)]),
        ("w0", w_hbm.at[0], w.at[0]), ("gain", gain_hbm, gain_in),
        ("spread", spread_hbm, spread), ("over", over_hbm, over), ("turns", turns_hbm, turns),
        ("waves", waves_hbm, waves), ("wout", wout_hbm, wout),
    ]):
        loads[name] = pltpu.make_async_copy(src, dst, load_sem.at[slot])
        loads[name].start()
        if name == "w2":
            each_peer(lambda peer: pl.semaphore_signal(barrier, inc=1, device_id={"ctx": peer}, device_id_type=MESH))
            for other in (partner, across, (1 - chip) * 2 + (1 - core)):
                pl.semaphore_signal(barrier, inc=1, device_id={"fft": other}, device_id_type=MESH)

    first_group = fft * (block // group_size)
    per_stream = taps_in.shape[1] // 3
    loads["taps"].wait()
    group_of = lax.broadcasted_iota(jnp.int32, (per_stream, block), 1) // group_size + first_group
    pick = (lax.broadcasted_iota(jnp.int32, (per_stream, block), 0) == group_of).astype(F32)
    blank = jnp.zeros((8 - n_taps, per_stream), F32)
    taps_rows = jnp.concatenate(
        [x for s in range(3) for x in (taps_in[:, s * per_stream:(s + 1) * per_stream], blank)], axis=0
    )
    taps_all = dot(taps_rows, pick, precision=lax.Precision.HIGHEST)

    def project(s, r0, r1):
        for n0 in range(0, block, min(256, block)):
            n1 = n0 + min(256, block)
            got = dot(tok[r0:r1, :], w[s, :, n0:n1])
            proj[s, RIM + r0:RIM + r1, n0:n1] = got.astype(BF16).astype(F32)

    def rim_copy(s):
        return pltpu.make_async_remote_copy(
            src_ref=proj.at[s, pl.ds(tok_len, RIM), :], dst_ref=proj.at[s, pl.ds(0, RIM), :],
            send_sem=rim_send_sem.at[s], recv_sem=rim_recv_sem.at[s],
            device_id={"ctx": lax.rem(me + 1, n_ctx)}, device_id_type=MESH,
        )

    def send_rim(s):
        @pl.when(me < n_ctx - 1)
        def _():
            rim_copy(s).start()

        @pl.when(me == 0)
        def _():
            proj[s, 0:RIM, :] = jnp.zeros((RIM, block), F32)

    def finish_rim(s):
        @pl.when(me > 0)
        def _():
            rim_copy(s).wait_recv()

    def featurize(s, t0, c0):
        window = proj[s, pl.ds(t0, tc + RIM), c0:c0 + lc]
        total = None
        for j in range(n_taps):
            term = taps_all[s * 8 + j:s * 8 + j + 1, c0:c0 + lc] * window[RIM - j:RIM - j + tc, :]
            total = term if total is None else total + term
        return total.astype(BF16).astype(F32)

    def mix(t0, c0):
        both = featurize(1, t0, c0) * featurize(2, t0, c0)
        mixed[pl.ds(t0, tc), c0:c0 + lc] = both
        turned = both.T.reshape(per_lc, stretch, tc).astype(BF16)
        send[c0 // stretch:c0 // stretch + per_lc, :, pl.ds(t0, tc)] = turned

    def exchange(source, target, send_sem, recv_sem):
        def copy_to(dest, h0, size, i):
            return pltpu.make_async_remote_copy(
                src_ref=source.at[dest, :, pl.ds(h0, size)], dst_ref=target.at[me, :, pl.ds(h0, size)],
                send_sem=send_sem.at[i], recv_sem=recv_sem.at[i],
                device_id={"ctx": dest}, device_id_type=MESH,
            )

        def start(h0, size, i):
            each_peer(lambda dest: copy_to(dest, h0, size, i).start())
            target[me, :, pl.ds(h0, size)] = source[me, :, pl.ds(h0, size)]

        def all_of(h0, size, i):
            return pltpu.make_async_remote_copy(
                src_ref=source.at[pl.ds(0, n_ctx - 1), :, pl.ds(h0, size)],
                dst_ref=target.at[pl.ds(0, n_ctx - 1), :, pl.ds(h0, size)],
                send_sem=send_sem.at[i], recv_sem=recv_sem.at[i],
                device_id={"ctx": lax.rem(me + 1, n_ctx)}, device_id_type=MESH,
            )

        return start, all_of

    go_start, go_all = exchange(send, recv, go_send_sem, go_recv_sem)

    loads["tok1"].wait()
    for s, name in ((1, "w1"), (2, "w2")):
        loads[name].wait()
        project(s, split, tok_len)
    for c0 in range(0, block, lc):
        @pl.loop(half // tc, tok_len // tc)
        def _(t):
            mix(pl.multiple_of(t * tc, tc), c0)

    loads["filt"].wait()
    flipped = filt[...].T.astype(BF16).astype(F32)
    lag_rows, lag_lanes = filt_send.shape[1:]
    for j in range(lag_rows):
        filt_send[:, j, :] = flipped[:, j * lag_lanes:(j + 1) * lag_lanes].astype(BF16)

    def filt_copy(dest):
        return pltpu.make_async_remote_copy(
            src_ref=filt_send.at[first_group + (dest * stretch) // group_size],
            dst_ref=filt_recv.at[me],
            send_sem=filt_sem.at[0], recv_sem=filt_sem.at[1],
            device_id={"ctx": dest}, device_id_type=MESH,
        )

    filt_all = pltpu.make_async_remote_copy(
        src_ref=filt_recv.at[pl.ds(0, n_ctx - 1)], dst_ref=filt_recv.at[pl.ds(0, n_ctx - 1)],
        send_sem=filt_sem.at[0], recv_sem=filt_sem.at[1],
        device_id={"ctx": lax.rem(me + 1, n_ctx)}, device_id_type=MESH,
    )
    filt_recv[me] = filt_send[first_group + (me * stretch) // group_size]

    pl.semaphore_wait(barrier, n_ctx - 1 + 3)
    send_rim(1)
    send_rim(2)
    go_start(half, half, 1)
    each_peer(lambda dest: filt_copy(dest).start())

    loads["tok0"].wait()
    project(1, 0, split)
    project(2, 0, split)
    for c0 in range(0, block, lc):
        @pl.loop(1, half // tc)
        def _(t):
            mix(pl.multiple_of(t * tc, tc), c0)

    finish_rim(1)
    finish_rim(2)
    for c0 in range(0, block, lc):
        mix(0, c0)
    go_start(0, half, 0)

    loads["w0"].wait()
    project(0, 0, tok_len)
    send_rim(0)
    loads["spread"].wait()
    spread_t[...] = spread[...].T

    kc = min(8, n_ctx)
    kr = kc * stretch
    mc = min(256, rows)

    def turned_by(table, re, im, m0, cols):
        n = re.shape[1]
        re = re.reshape(-1, stretch, n)
        im = im.reshape(-1, stretch, n)
        k0 = m0 // stretch
        b_re = table[0, k0:k0 + re.shape[0], cols][:, None, :]
        b_im = table[1, k0:k0 + re.shape[0], cols][:, None, :]
        return re, im, b_re, b_im

    loads["turns"].wait()

    def first_stage(h0):
        @pl.loop(0, n_ctx // kc)
        def _(i):
            got = recv[pl.ds(i * kc, kc), :, h0:h0 + half].astype(F32)
            signal[pl.ds(pl.multiple_of(i * kr, kr), kr), h0:h0 + half] = got.reshape(kr, half).astype(BF16)

        for m0 in range(0, rows, mc):
            re, im, b_re, b_im = turned_by(
                turns, dot(spread[m0:m0 + mc, :], signal[:, h0:h0 + half]),
                dot(spread[rows + m0:rows + m0 + mc, :], signal[:, h0:h0 + half]), m0, pl.ds(h0, half))
            o_re = (re * b_re - im * b_im).reshape(mc, half)
            o_im = (re * b_im + im * b_re).reshape(mc, half)
            lhs[m0:m0 + mc, h0:h0 + half] = o_re.astype(BF16)
            lhs[m0:m0 + mc, tok_len + h0:tok_len + h0 + half] = o_im.astype(BF16)
            lhs[rows + m0:rows + m0 + mc, h0:h0 + half] = o_im.astype(BF16)
            lhs[rows + m0:rows + m0 + mc, tok_len + h0:tok_len + h0 + half] = (-o_re).astype(BF16)

    loads["over"].wait()
    loads["waves"].wait()
    filt_all.wait_recv()
    lags3 = filt_recv[...].astype(F32)
    lags = jnp.concatenate([lags3[:, j, :] for j in range(lag_rows)], axis=1).astype(BF16)
    first = dot(over[...].astype(BF16), lags)
    f_re, f_im = first[:n_ctx], first[n_ctx:]
    t_re, t_im = turns[0], turns[1]
    g_re = (f_re * t_re - f_im * t_im).astype(BF16)
    g_im = (f_re * t_im + f_im * t_re).astype(BF16)
    top = jnp.concatenate([g_re, g_im], axis=1)
    bottom = jnp.concatenate([g_im, -g_re], axis=1)
    scale = 1.0 / (n_ctx * tok_len)
    spec[0] = dot(top, waves[...]) * scale
    spec[1] = dot(bottom, waves[...]) * scale

    go_all(half, half, 1).wait_recv()
    first_stage(half)

    go_all(0, half, 0).wait_recv()
    first_stage(0)

    for m0 in range(0, rows, mc):
        re, im, b_re, b_im = turned_by(
            spec, dot(lhs[m0:m0 + mc, :], waves[...]), dot(lhs[rows + m0:rows + m0 + mc, :], waves[...]),
            m0, slice(None))
        o_re = (re * b_re - im * b_im).reshape(mc, tok_len)
        o_im = (re * b_im + im * b_re).reshape(mc, tok_len)
        lhs2[m0:m0 + mc, :tok_len] = o_re.astype(BF16)
        lhs2[m0:m0 + mc, tok_len:] = (-o_im).astype(BF16)
        lhs2[rows + m0:rows + m0 + mc, :tok_len] = o_im.astype(BF16)
        lhs2[rows + m0:rows + m0 + mc, tok_len:] = o_re.astype(BF16)

    come_start, come_all = exchange(send2, recv2, come_send_sem, come_recv_sem)

    def last_stage(h0):
        cols = pl.ds(h0, half)
        for m0 in range(0, rows, mc):
            re, im, b_re, b_im = turned_by(
                turns, dot(lhs2[m0:m0 + mc, :], waves[:, cols]),
                dot(lhs2[rows + m0:rows + m0 + mc, :], waves[:, cols]), m0, cols)
            back[m0:m0 + mc, :] = (re * b_re + im * b_im).reshape(mc, half).astype(BF16)
            back[rows + m0:rows + m0 + mc, :] = (im * b_re - re * b_im).reshape(mc, half).astype(BF16)

        for m0 in range(0, rows, mc):
            got = dot(spread_t[m0:m0 + mc, :], back[...])
            send2[m0 // stretch:(m0 + mc) // stretch, :, cols] = (
                got.reshape(mc // stretch, stretch, half).astype(BF16))

    theirs = (1 - chip) * half
    ours = pl.multiple_of(chip * half, half)
    parts = [pl.multiple_of(theirs + j * piece, piece) for j in range(2)]
    last_stage(pl.multiple_of(theirs, half))
    come_start(parts[0], piece, 0)
    come_start(parts[1], piece, 1)
    last_stage(ours)
    come_start(ours, half, 2)

    finish_rim(0)
    for c0 in range(0, block, lc):
        @pl.loop(0, tok_len // tc)
        def _(t):
            t0 = pl.multiple_of(t * tc, tc)
            query[pl.ds(t0, tc), c0:c0 + lc] = featurize(0, t0, c0)

    loads["wout"].wait()
    loads["gain"].wait()
    gain_row = gain_in[:, pl.ds(pl.multiple_of(fft * block, block), block)]
    n_chunks, oc = part.shape[0], part.shape[2]
    share = n_chunks // 2
    gc = min(128, piece)

    def gate(h0, size):
        for c0 in range(0, block, lc):
            for t in range(0, size, gc):
                t0 = pl.multiple_of(h0 + t, gc)
                got = recv2[c0 // stretch:c0 // stretch + per_lc, :, pl.ds(t0, gc)].astype(F32)
                conv = got.reshape(lc, gc).T
                whole = conv + gain_row[:, c0:c0 + lc] * mixed[pl.ds(t0, gc), c0:c0 + lc]
                gated[pl.ds(t0, gc), c0:c0 + lc] = (query[pl.ds(t0, gc), c0:c0 + lc] * whole).astype(BF16)

    def pair_copy(n):
        return pltpu.make_async_remote_copy(
            src_ref=pair_send.at[n], dst_ref=pair_recv.at[n],
            send_sem=pair_send_sem.at[n], recv_sem=pair_recv_sem.at[n],
            device_id={"fft": partner}, device_id_type=MESH,
        )

    def cross_copy(j, i):
        n = core * share + i
        return pltpu.make_async_remote_copy(
            src_ref=cross_send.at[j, i], dst_ref=cross_out.at[:, pl.ds(pl.multiple_of(n * oc, oc), oc)],
            send_sem=cross_send_sem.at[j, i], recv_sem=cross_recv_sem.at[n],
            device_id={"fft": (1 - chip) * 2 + j}, device_id_type=MESH,
        )

    def cross_arrival(n):
        return pltpu.make_async_remote_copy(
            src_ref=cross_send.at[0, 0], dst_ref=cross_out.at[:, n * oc:(n + 1) * oc],
            send_sem=cross_send_sem.at[0, 0], recv_sem=cross_recv_sem.at[n],
            device_id={"fft": across}, device_id_type=MESH,
        )

    def product(h0, size, n):
        return dot(gated[pl.ds(h0, size), :], wout[:, pl.ds(pl.multiple_of(n * oc, oc), oc)])

    go_all(half, half, 1).wait_send()
    go_all(0, half, 0).wait_send()
    filt_all.wait_send()

    @pl.when(me < n_ctx - 1)
    def _():
        for s in range(3):
            rim_copy(s).wait_send()

    for j in range(2):
        come_all(parts[j], piece, j).wait_recv()
        gate(parts[j], piece)
        for i in range(share):
            pair_send[j * share + i] = product(parts[j], piece, (1 - core) * share + i).astype(BF16)
            pair_copy(j * share + i).start()
        for i in range(share):
            part[i, 0:piece, :] = product(parts[j], piece, core * share + i)
        for i in range(share):
            pair_copy(j * share + i).wait_recv()
            cross_send[j, i] = (part[i, 0:piece, :] + pair_recv[j * share + i].astype(F32)).astype(BF16)
            cross_copy(j, i).start()

    come_all(ours, half, 2).wait_recv()
    gate(ours, half)
    for n in range(n_chunks):
        part[n] = product(ours, half, n)
        other = part[n, pl.ds(pl.multiple_of((1 - core) * piece, piece), piece), :]
        pair_send[n_chunks + n] = other.astype(BF16)
        pair_copy(n_chunks + n).start()
    for n in range(n_chunks):
        pair_copy(n_chunks + n).wait_recv()
        mine = part[n, pl.ds(pl.multiple_of(core * piece, piece), piece), :]
        kept[:, n * oc:(n + 1) * oc] = mine + pair_recv[n_chunks + n].astype(F32)
    keep = pltpu.make_async_copy(kept, kept_out, load_sem.at[0])
    keep.start()

    come_all(parts[0], piece, 0).wait_send()
    come_all(parts[1], piece, 1).wait_send()
    come_all(ours, half, 2).wait_send()
    for n in range(2 * n_chunks):
        pair_copy(n).wait_send()
    keep.wait()
    for n in range(n_chunks):
        cross_arrival(n).wait_recv()
    for j in range(2):
        for i in range(share):
            cross_copy(j, i).wait_send()


def body(tokens, w_in, short_taps, long_filter, skip_gain, w_out):
    n_ctx = lax.axis_size("ctx")
    n_fft = lax.axis_size("fft")
    tok_len, width = tokens.shape
    block = w_in.shape[2]
    n_groups = long_filter.shape[1]
    group_size = width // n_groups
    stretch = block // n_ctx
    rows = n_ctx * stretch
    piece = tok_len // n_fft
    oc = min(512, width // 4)
    n_chunks = width // oc
    lag_rows = 4
    over, spread, turns, waves = tables(n_ctx, tok_len, stretch)
    dma = pltpu.SemaphoreType.DMA
    vmem = pltpu.VMEM
    streams = w_in.transpose(1, 0, 2)
    args = (
        tokens, streams, short_taps, long_filter, skip_gain.reshape(1, width), w_out,
        jnp.asarray(over), jnp.asarray(spread), jnp.asarray(turns), jnp.asarray(waves),
    )
    kept, crossed = pl.pallas_call(
        functools.partial(kernel, n_ctx, n_fft, group_size),
        out_shape=(jax.ShapeDtypeStruct((piece, width), F32), jax.ShapeDtypeStruct((piece, width), BF16)),
        in_specs=[pl.BlockSpec(memory_space=pl.ANY)] * len(args),
        out_specs=(pl.BlockSpec(memory_space=pl.ANY), pl.BlockSpec(memory_space=pl.ANY)),
        scratch_shapes=[vmem(a.shape, a.dtype) for a in args] + [
            vmem((rows, 2 * rows), BF16),
            vmem((3, tok_len + RIM, block), F32),
            vmem((tok_len, block), F32),
            vmem((tok_len, block), F32),
            vmem((n_ctx, stretch, tok_len), BF16),
            vmem((n_ctx, stretch, tok_len), BF16),
            vmem((n_groups, lag_rows, tok_len // lag_rows), BF16),
            vmem((n_ctx, lag_rows, tok_len // lag_rows), BF16),
            vmem((rows, tok_len), BF16),
            vmem((2 * rows, 2 * tok_len), BF16),
            vmem((2 * rows, 2 * tok_len), BF16),
            vmem((2, n_ctx, tok_len), F32),
            vmem((2 * rows, tok_len // 2), BF16),
            vmem((n_ctx, stretch, tok_len), BF16),
            vmem((n_ctx, stretch, tok_len), BF16),
            vmem((tok_len, block), BF16),
            vmem((n_chunks, tok_len // 2, oc), F32),
            vmem((piece, width), F32),
            vmem((2 * n_chunks, piece, oc), BF16),
            vmem((2 * n_chunks, piece, oc), BF16),
            vmem((2, n_chunks // 2, piece, oc), BF16),
            dma((13,)), dma((3,)), dma((3,)), dma((2,)), dma((2,)), dma((2,)), dma((3,)), dma((3,)),
            dma((2 * n_chunks,)), dma((2 * n_chunks,)), dma((2, n_chunks // 2)), dma((n_chunks,)),
        ],
        compiler_params=pltpu.CompilerParams(
            collective_id=0, has_side_effects=True, vmem_limit_bytes=60 * 1024 * 1024
        ),
        name="hyena",
    )(*args)
    return (kept + crossed.astype(F32)).astype(BF16)


def solution(mesh):
    return jax.shard_map(
        body,
        mesh=mesh,
        in_specs=(P("ctx", None), P(None, None, "fft"), P(), P("ctx", None), P(), P("fft", None)),
        out_specs=P(("ctx", "fft"), None),
        check_vma=False,
    )
```

```python
import functools
import math

import jax
import jax.numpy as jnp
import numpy as np
from jax import lax
from jax.experimental import pallas as pl
from jax.experimental.pallas import tpu as pltpu
from jax.sharding import PartitionSpec as P

MESH = pl.DeviceIdType.MESH
F32 = jnp.float32
BF16 = jnp.bfloat16
RIM = 8


def tables(n_ctx, tok_len, stretch):
    blocks = np.arange(n_ctx)
    lags = np.arange(tok_len)
    odd = 2 * blocks + 1
    angle = (odd[:, None] * blocks[None, :] % (4 * n_ctx)) * (2.0 * math.pi / (4 * n_ctx))
    eye = np.eye(stretch)
    over_blocks = np.concatenate([np.cos(angle), -np.sin(angle)], axis=0)
    spread = np.kron(over_blocks, eye)
    turn = (odd[:, None] * lags[None, :]) * (2.0 * math.pi / (4 * n_ctx * tok_len))
    turns = np.stack([np.cos(turn), -np.sin(turn)])
    inner = (lags[:, None] * lags[None, :] % tok_len) * (2.0 * math.pi / tok_len)
    waves = np.concatenate([np.cos(inner), np.sin(inner)], axis=0)
    return (
        over_blocks.astype(np.float32),
        spread.astype(np.float32).astype(jnp.bfloat16),
        turns.astype(np.float32),
        waves.astype(np.float32).astype(jnp.bfloat16),
    )


def dot(a, b, **kw):
    return jnp.dot(a, b, preferred_element_type=F32, **kw)


def kernel(
    n_ctx, n_fft, group_size,
    tok_hbm, w_hbm, taps_hbm, filt_hbm, gain_hbm, wout_hbm, over_hbm, spread_hbm, turns_hbm, waves_hbm,
    kept_out, cross_out,
    tok, w, taps_in, filt, gain_in, wout, over, spread, turns, waves,
    spread_t, proj, mixed, query, send, recv, filt_send, filt_recv,
    signal, lhs, lhs2, spec, back, send2, recv2, gated, part, kept,
    pair_send, pair_recv, cross_send, twin_query, twin_mixed,
    load_sem, rim_send_sem, rim_recv_sem, filt_sem, go_send_sem, go_recv_sem, come_send_sem, come_recv_sem,
    pair_send_sem, pair_recv_sem, cross_send_sem, cross_recv_sem, twin_sem,
):
    me = lax.axis_index("ctx")
    fft = lax.axis_index("fft")
    chip = fft // 2
    core = fft % 2
    twin = me + 1 - 2 * (me % 2)
    partner = chip * 2 + (1 - core)
    across = (1 - chip) * 2 + core
    tok_len, width = tok.shape
    block = w.shape[2]
    stretch = block // n_ctx
    rows = n_ctx * stretch
    n_taps = taps_in.shape[0]
    piece = tok_len // n_fft
    half = tok_len // 2
    tc = min(128, half)
    lc = min(128, block)
    per_lc = lc // stretch

    barrier = pltpu.get_barrier_semaphore()

    def each_peer(act):
        group = next(g for g in (9, 7, 5, 3, 1) if (n_ctx - 1) % g == 0)

        @pl.loop(0, (n_ctx - 1) // group)
        def _(i):
            for j in range(group):
                m = n_ctx - 1 - j - i * group
                d = (m + 1) // 2
                odd = m % 2
                act(lax.rem(me + odd * d + (1 - odd) * (n_ctx - d), n_ctx))

    split = half - 16
    loads = {}
    for slot, (name, src, dst) in enumerate([
        ("taps", taps_hbm, taps_in),
        ("tok1", tok_hbm.at[pl.ds(split, tok_len - split)], tok.at[pl.ds(split, tok_len - split)]),
        ("w1", w_hbm.at[1], w.at[1]), ("w2", w_hbm.at[2], w.at[2]),
        ("filt", filt_hbm, filt), ("tok0", tok_hbm.at[pl.ds(0, split)], tok.at[pl.ds(0, split)]),
        ("w0", w_hbm.at[0], w.at[0]), ("gain", gain_hbm, gain_in),
        ("spread", spread_hbm, spread), ("over", over_hbm, over), ("turns", turns_hbm, turns),
        ("waves", waves_hbm, waves), ("wout", wout_hbm, wout),
    ]):
        loads[name] = pltpu.make_async_copy(src, dst, load_sem.at[slot])
        loads[name].start()
        if name == "w2":
            each_peer(lambda peer: pl.semaphore_signal(barrier, inc=1, device_id={"ctx": peer}, device_id_type=MESH))
            for other in (partner, across, (1 - chip) * 2 + (1 - core)):
                pl.semaphore_signal(barrier, inc=1, device_id={"fft": other}, device_id_type=MESH)
            for k in range(2):
                pl.semaphore_signal(
                    barrier, inc=1, device_id={"ctx": twin, "fft": (1 - chip) * 2 + k}, device_id_type=MESH)

    first_group = fft * (block // group_size)
    per_stream = taps_in.shape[1] // 3
    loads["taps"].wait()
    group_of = lax.broadcasted_iota(jnp.int32, (per_stream, block), 1) // group_size + first_group
    pick = (lax.broadcasted_iota(jnp.int32, (per_stream, block), 0) == group_of).astype(F32)
    blank = jnp.zeros((8 - n_taps, per_stream), F32)
    taps_rows = jnp.concatenate(
        [x for s in range(3) for x in (taps_in[:, s * per_stream:(s + 1) * per_stream], blank)], axis=0
    )
    taps_all = dot(taps_rows, pick, precision=lax.Precision.HIGHEST)

    def project(s, r0, r1):
        for n0 in range(0, block, min(256, block)):
            n1 = n0 + min(256, block)
            got = dot(tok[r0:r1, :], w[s, :, n0:n1])
            got = got.astype(BF16).astype(F32)
            for c0 in range(n0, n1, lc):
                proj[s, c0 // lc, RIM + r0:RIM + r1, :] = got[:, c0 - n0:c0 - n0 + lc]

    def rim_copy(s):
        return pltpu.make_async_remote_copy(
            src_ref=proj.at[s, :, pl.ds(tok_len, RIM), :], dst_ref=proj.at[s, :, pl.ds(0, RIM), :],
            send_sem=rim_send_sem.at[s], recv_sem=rim_recv_sem.at[s],
            device_id={"ctx": lax.rem(me + 1, n_ctx)}, device_id_type=MESH,
        )

    def send_rim(s):
        @pl.when(me < n_ctx - 1)
        def _():
            rim_copy(s).start()

        @pl.when(me == 0)
        def _():
            proj[s, :, 0:RIM, :] = jnp.zeros((block // lc, RIM, lc), F32)

    def finish_rim(s):
        @pl.when(me > 0)
        def _():
            rim_copy(s).wait_recv()

    def featurize(s, t0, c0):
        total = None
        for j in range(n_taps):
            term = taps_all[s * 8 + j:s * 8 + j + 1, c0:c0 + lc] * proj[s, c0 // lc, pl.ds(t0 + (RIM - j), tc), :]
            total = term if total is None else total + term
        return total.astype(BF16).astype(F32)

    def mix(t0, c0):
        both = featurize(1, t0, c0) * featurize(2, t0, c0)
        mixed[pl.ds(t0, tc), c0:c0 + lc] = both
        turned = both.T.reshape(per_lc, stretch, tc).astype(BF16)
        send[c0 // stretch:c0 // stretch + per_lc, :, pl.ds(t0, tc)] = turned

    def exchange(source, target, send_sem, recv_sem):
        def held_for(dest, crossed):
            return dest + 1 - 2 * (dest % 2) if crossed else dest

        def copy_to(dest, h0, size, i, crossed):
            return pltpu.make_async_remote_copy(
                src_ref=source.at[held_for(dest, crossed), :, pl.ds(h0, size)],
                dst_ref=target.at[me, :, pl.ds(h0, size)],
                send_sem=send_sem.at[i], recv_sem=recv_sem.at[i],
                device_id={"ctx": dest}, device_id_type=MESH,
            )

        def start(h0, size, i, crossed=False):
            each_peer(lambda dest: copy_to(dest, h0, size, i, crossed).start())
            target[me, :, pl.ds(h0, size)] = source[held_for(me, crossed), :, pl.ds(h0, size)]

        def all_of(h0, size, i):
            return pltpu.make_async_remote_copy(
                src_ref=source.at[pl.ds(0, n_ctx - 1), :, pl.ds(h0, size)],
                dst_ref=target.at[pl.ds(0, n_ctx - 1), :, pl.ds(h0, size)],
                send_sem=send_sem.at[i], recv_sem=recv_sem.at[i],
                device_id={"ctx": lax.rem(me + 1, n_ctx)}, device_id_type=MESH,
            )

        return start, all_of

    go_start, go_all = exchange(send, recv, go_send_sem, go_recv_sem)

    loads["tok1"].wait()
    for s, name in ((1, "w1"), (2, "w2")):
        loads[name].wait()
        project(s, split, tok_len)
    for c0 in range(0, block, lc):
        @pl.loop(half // tc, tok_len // tc)
        def _(t):
            mix(pl.multiple_of(t * tc, tc), c0)

    loads["filt"].wait()
    flipped = filt[...].T.astype(BF16).astype(F32)
    lag_rows, lag_lanes = filt_send.shape[1:]
    for j in range(lag_rows):
        filt_send[:, j, :] = flipped[:, j * lag_lanes:(j + 1) * lag_lanes].astype(BF16)

    def filt_copy(dest):
        return pltpu.make_async_remote_copy(
            src_ref=filt_send.at[first_group + (dest * stretch) // group_size],
            dst_ref=filt_recv.at[me],
            send_sem=filt_sem.at[0], recv_sem=filt_sem.at[1],
            device_id={"ctx": dest}, device_id_type=MESH,
        )

    filt_all = pltpu.make_async_remote_copy(
        src_ref=filt_recv.at[pl.ds(0, n_ctx - 1)], dst_ref=filt_recv.at[pl.ds(0, n_ctx - 1)],
        send_sem=filt_sem.at[0], recv_sem=filt_sem.at[1],
        device_id={"ctx": lax.rem(me + 1, n_ctx)}, device_id_type=MESH,
    )
    filt_recv[me] = filt_send[first_group + (me * stretch) // group_size]

    pl.semaphore_wait(barrier, n_ctx - 1 + 3 + 2)
    send_rim(1)
    send_rim(2)
    go_start(half, half, 1)
    each_peer(lambda dest: filt_copy(dest).start())

    loads["tok0"].wait()
    project(1, 0, split)
    project(2, 0, split)
    for c0 in range(0, block, lc):
        @pl.loop(1, half // tc)
        def _(t):
            mix(pl.multiple_of(t * tc, tc), c0)

    finish_rim(1)
    finish_rim(2)
    for c0 in range(0, block, lc):
        mix(0, c0)
    go_start(0, half, 0)

    loads["w0"].wait()
    project(0, 0, tok_len)
    send_rim(0)
    loads["spread"].wait()
    spread_t[...] = spread[...].T

    kc = min(8, n_ctx)
    kr = kc * stretch
    mc = min(256, rows)

    def turned_by(table, re, im, m0, cols):
        n = re.shape[1]
        re = re.reshape(-1, stretch, n)
        im = im.reshape(-1, stretch, n)
        k0 = m0 // stretch
        b_re = table[0, k0:k0 + re.shape[0], cols][:, None, :]
        b_im = table[1, k0:k0 + re.shape[0], cols][:, None, :]
        return re, im, b_re, b_im

    loads["turns"].wait()

    def first_stage(h0):
        @pl.loop(0, n_ctx // kc)
        def _(i):
            got = recv[pl.ds(i * kc, kc), :, h0:h0 + half].astype(F32)
            signal[pl.ds(pl.multiple_of(i * kr, kr), kr), h0:h0 + half] = got.reshape(kr, half).astype(BF16)

        for m0 in range(0, rows, mc):
            re, im, b_re, b_im = turned_by(
                turns, dot(spread[m0:m0 + mc, :], signal[:, h0:h0 + half]),
                dot(spread[rows + m0:rows + m0 + mc, :], signal[:, h0:h0 + half]), m0, pl.ds(h0, half))
            o_re = (re * b_re - im * b_im).reshape(mc, half)
            o_im = (re * b_im + im * b_re).reshape(mc, half)
            lhs[m0:m0 + mc, h0:h0 + half] = o_re.astype(BF16)
            lhs[m0:m0 + mc, tok_len + h0:tok_len + h0 + half] = o_im.astype(BF16)
            lhs[rows + m0:rows + m0 + mc, h0:h0 + half] = o_im.astype(BF16)
            lhs[rows + m0:rows + m0 + mc, tok_len + h0:tok_len + h0 + half] = (-o_re).astype(BF16)

    loads["over"].wait()
    loads["waves"].wait()
    filt_all.wait_recv()
    lags3 = filt_recv[...].astype(F32)
    lags = jnp.concatenate([lags3[:, j, :] for j in range(lag_rows)], axis=1).astype(BF16)
    first = dot(over[...].astype(BF16), lags)
    f_re, f_im = first[:n_ctx], first[n_ctx:]
    t_re, t_im = turns[0], turns[1]
    g_re = (f_re * t_re - f_im * t_im).astype(BF16)
    g_im = (f_re * t_im + f_im * t_re).astype(BF16)
    top = jnp.concatenate([g_re, g_im], axis=1)
    bottom = jnp.concatenate([g_im, -g_re], axis=1)
    scale = 1.0 / (n_ctx * tok_len)
    spec[0] = dot(top, waves[...]) * scale
    spec[1] = dot(bottom, waves[...]) * scale

    go_all(half, half, 1).wait_recv()
    first_stage(half)

    finish_rim(0)
    for c0 in range(0, block, lc):
        @pl.loop(0, tok_len // tc)
        def _(t):
            t0 = pl.multiple_of(t * tc, tc)
            query[pl.ds(t0, tc), c0:c0 + lc] = featurize(0, t0, c0).astype(BF16)

    theirs = (1 - chip) * half
    ours = pl.multiple_of(chip * half, half)
    parts = [pl.multiple_of(theirs + j * piece, piece) for j in range(2)]
    twin_mixed[0] = mixed[pl.ds(parts[1], piece), :].astype(BF16)

    def twin_copy(i):
        return pltpu.make_async_remote_copy(
            src_ref=(query.at[pl.ds(parts[1], piece)], twin_mixed.at[0])[i],
            dst_ref=(twin_query, twin_mixed.at[1])[i],
            send_sem=twin_sem.at[0, i], recv_sem=twin_sem.at[1, i],
            device_id={"ctx": twin}, device_id_type=MESH,
        )

    twin_copy(0).start()
    twin_copy(1).start()

    go_all(0, half, 0).wait_recv()
    first_stage(0)

    for m0 in range(0, rows, mc):
        re, im, b_re, b_im = turned_by(
            spec, dot(lhs[m0:m0 + mc, :], waves[...]), dot(lhs[rows + m0:rows + m0 + mc, :], waves[...]),
            m0, slice(None))
        o_re = (re * b_re - im * b_im).reshape(mc, tok_len)
        o_im = (re * b_im + im * b_re).reshape(mc, tok_len)
        lhs2[m0:m0 + mc, :tok_len] = o_re.astype(BF16)
        lhs2[m0:m0 + mc, tok_len:] = (-o_im).astype(BF16)
        lhs2[rows + m0:rows + m0 + mc, :tok_len] = o_im.astype(BF16)
        lhs2[rows + m0:rows + m0 + mc, tok_len:] = o_re.astype(BF16)

    come_start, come_all = exchange(send2, recv2, come_send_sem, come_recv_sem)

    def last_stage(h0, size):
        cols = pl.ds(h0, size)
        for m0 in range(0, rows, mc):
            re, im, b_re, b_im = turned_by(
                turns, dot(lhs2[m0:m0 + mc, :], waves[:, cols]),
                dot(lhs2[rows + m0:rows + m0 + mc, :], waves[:, cols]), m0, cols)
            back[m0:m0 + mc, :size] = (re * b_re + im * b_im).reshape(mc, size).astype(BF16)
            back[rows + m0:rows + m0 + mc, :size] = (im * b_re - re * b_im).reshape(mc, size).astype(BF16)

        for m0 in range(0, rows, mc):
            got = dot(spread_t[m0:m0 + mc, :], back[:, :size])
            send2[m0 // stretch:(m0 + mc) // stretch, :, cols] = (
                got.reshape(mc // stretch, stretch, size).astype(BF16))

    for j in range(2):
        last_stage(parts[j], piece)
        come_start(parts[j], piece, j, crossed=j == 1)
    last_stage(ours, half)
    come_start(ours, half, 2)

    loads["wout"].wait()
    loads["gain"].wait()
    gain_row = gain_in[:, pl.ds(pl.multiple_of(fft * block, block), block)]
    n_chunks, oc = part.shape[0], part.shape[2]
    share = n_chunks // 2
    gc = min(128, piece)

    def gate(h0, size, asked, direct, off):
        for c0 in range(0, block, lc):
            for t in range(0, size, gc):
                t0 = pl.multiple_of(h0 + t, gc)
                got = recv2[c0 // stretch:c0 // stretch + per_lc, :, pl.ds(t0, gc)].astype(F32)
                conv = got.reshape(lc, gc).T
                at = pl.multiple_of(off + t, gc)
                whole = conv + gain_row[:, c0:c0 + lc] * direct[pl.ds(at, gc), c0:c0 + lc].astype(F32)
                gated[pl.ds(t0, gc), c0:c0 + lc] = (
                    asked[pl.ds(at, gc), c0:c0 + lc].astype(F32) * whole).astype(BF16)

    def pair_copy(n):
        return pltpu.make_async_remote_copy(
            src_ref=pair_send.at[n], dst_ref=pair_recv.at[n],
            send_sem=pair_send_sem.at[n], recv_sem=pair_recv_sem.at[n],
            device_id={"fft": partner}, device_id_type=MESH,
        )

    def cross_copy(j, i):
        n = core * share + i
        return pltpu.make_async_remote_copy(
            src_ref=cross_send.at[j, i], dst_ref=cross_out.at[:, pl.ds(pl.multiple_of(n * oc, oc), oc)],
            send_sem=cross_send_sem.at[j, i], recv_sem=cross_recv_sem.at[n],
            device_id={"ctx": twin if j else me, "fft": (1 - chip) * 2 + j}, device_id_type=MESH,
        )

    def cross_arrival(n):
        return pltpu.make_async_remote_copy(
            src_ref=cross_send.at[0, 0], dst_ref=cross_out.at[:, n * oc:(n + 1) * oc],
            send_sem=cross_send_sem.at[0, 0], recv_sem=cross_recv_sem.at[n],
            device_id={"fft": across}, device_id_type=MESH,
        )

    def product(h0, size, n):
        return dot(gated[pl.ds(h0, size), :], wout[:, pl.ds(pl.multiple_of(n * oc, oc), oc)])

    go_all(half, half, 1).wait_send()
    go_all(0, half, 0).wait_send()
    filt_all.wait_send()

    @pl.when(me < n_ctx - 1)
    def _():
        for s in range(3):
            rim_copy(s).wait_send()

    for j in range(2):
        come_all(parts[j], piece, j).wait_recv()
        if j == 0:
            gate(parts[j], piece, query, mixed, parts[j])
        else:
            twin_copy(0).wait_recv()
            twin_copy(1).wait_recv()
            gate(parts[j], piece, twin_query, twin_mixed.at[1], 0)
        for i in range(share):
            pair_send[j * share + i] = product(parts[j], piece, (1 - core) * share + i).astype(BF16)
            pair_copy(j * share + i).start()
        for i in range(share):
            part[i, 0:piece, :] = product(parts[j], piece, core * share + i)
        for i in range(share):
            pair_copy(j * share + i).wait_recv()
            cross_send[j, i] = (part[i, 0:piece, :] + pair_recv[j * share + i].astype(F32)).astype(BF16)
            cross_copy(j, i).start()

    come_all(ours, half, 2).wait_recv()
    gate(ours, half, query, mixed, ours)
    for n in range(n_chunks):
        part[n] = product(ours, half, n)
        other = part[n, pl.ds(pl.multiple_of((1 - core) * piece, piece), piece), :]
        pair_send[n_chunks + n] = other.astype(BF16)
        pair_copy(n_chunks + n).start()
    for n in range(n_chunks):
        pair_copy(n_chunks + n).wait_recv()
        mine = part[n, pl.ds(pl.multiple_of(core * piece, piece), piece), :]
        kept[:, n * oc:(n + 1) * oc] = mine + pair_recv[n_chunks + n].astype(F32)
    keep = pltpu.make_async_copy(kept, kept_out, load_sem.at[0])
    keep.start()

    come_all(parts[0], piece, 0).wait_send()
    come_all(parts[1], piece, 1).wait_send()
    come_all(ours, half, 2).wait_send()
    for n in range(2 * n_chunks):
        pair_copy(n).wait_send()
    keep.wait()
    twin_copy(0).wait_send()
    twin_copy(1).wait_send()
    for n in range(n_chunks):
        cross_arrival(n).wait_recv()
    for j in range(2):
        for i in range(share):
            cross_copy(j, i).wait_send()


def body(tokens, w_in, short_taps, long_filter, skip_gain, w_out):
    n_ctx = lax.axis_size("ctx")
    n_fft = lax.axis_size("fft")
    tok_len, width = tokens.shape
    block = w_in.shape[2]
    n_groups = long_filter.shape[1]
    group_size = width // n_groups
    stretch = block // n_ctx
    rows = n_ctx * stretch
    piece = tok_len // n_fft
    oc = min(512, width // 4)
    n_chunks = width // oc
    lag_rows = 4
    lc = min(128, block)
    over, spread, turns, waves = tables(n_ctx, tok_len, stretch)
    dma = pltpu.SemaphoreType.DMA
    vmem = pltpu.VMEM
    streams = w_in.transpose(1, 0, 2)
    args = (
        tokens, streams, short_taps, long_filter, skip_gain.reshape(1, width), w_out,
        jnp.asarray(over), jnp.asarray(spread), jnp.asarray(turns), jnp.asarray(waves),
    )
    kept, crossed = pl.pallas_call(
        functools.partial(kernel, n_ctx, n_fft, group_size),
        out_shape=(jax.ShapeDtypeStruct((piece, width), F32), jax.ShapeDtypeStruct((piece, width), BF16)),
        in_specs=[pl.BlockSpec(memory_space=pl.ANY)] * len(args),
        out_specs=(pl.BlockSpec(memory_space=pl.ANY), pl.BlockSpec(memory_space=pl.ANY)),
        scratch_shapes=[vmem(a.shape, a.dtype) for a in args] + [
            vmem((rows, 2 * rows), BF16),
            vmem((3, block // lc, tok_len + RIM, lc), F32),
            vmem((tok_len, block), F32),
            vmem((tok_len, block), BF16),
            vmem((n_ctx, stretch, tok_len), BF16),
            vmem((n_ctx, stretch, tok_len), BF16),
            vmem((n_groups, lag_rows, tok_len // lag_rows), BF16),
            vmem((n_ctx, lag_rows, tok_len // lag_rows), BF16),
            vmem((rows, tok_len), BF16),
            vmem((2 * rows, 2 * tok_len), BF16),
            vmem((2 * rows, 2 * tok_len), BF16),
            vmem((2, n_ctx, tok_len), F32),
            vmem((2 * rows, tok_len // 2), BF16),
            vmem((n_ctx, stretch, tok_len), BF16),
            vmem((n_ctx, stretch, tok_len), BF16),
            vmem((tok_len, block), BF16),
            vmem((n_chunks, tok_len // 2, oc), F32),
            vmem((piece, width), F32),
            vmem((2 * n_chunks, piece, oc), BF16),
            vmem((2 * n_chunks, piece, oc), BF16),
            vmem((2, n_chunks // 2, piece, oc), BF16),
            vmem((piece, block), BF16),
            vmem((2, piece, block), BF16),
            dma((13,)), dma((3,)), dma((3,)), dma((2,)), dma((2,)), dma((2,)), dma((3,)), dma((3,)),
            dma((2 * n_chunks,)), dma((2 * n_chunks,)), dma((2, n_chunks // 2)), dma((n_chunks,)), dma((2, 2)),
        ],
        compiler_params=pltpu.CompilerParams(
            collective_id=0, has_side_effects=True, vmem_limit_bytes=60 * 1024 * 1024
        ),
        name="hyena",
    )(*args)
    return (kept + crossed.astype(F32)).astype(BF16)


def solution(mesh):
    return jax.shard_map(
        body,
        mesh=mesh,
        in_specs=(P("ctx", None), P(None, None, "fft"), P(), P("ctx", None), P(), P("fft", None)),
        out_specs=P(("ctx", "fft"), None),
        check_vma=False,
    )
```

```python
import functools
import math

import jax
import jax.numpy as jnp
import numpy as np
from jax import lax
from jax.experimental import pallas as pl
from jax.experimental.pallas import tpu as pltpu
from jax.sharding import PartitionSpec as P

MESH = pl.DeviceIdType.MESH
F32 = jnp.float32
BF16 = jnp.bfloat16
RIM = 8


def tables(n_ctx, tok_len, stretch):
    blocks = np.arange(n_ctx)
    lags = np.arange(tok_len)
    odd = 2 * blocks + 1
    angle = (odd[:, None] * blocks[None, :] % (4 * n_ctx)) * (2.0 * math.pi / (4 * n_ctx))
    eye = np.eye(stretch)
    over_blocks = np.concatenate([np.cos(angle), -np.sin(angle)], axis=0)
    spread = np.kron(over_blocks, eye)
    turn = (odd[:, None] * lags[None, :]) * (2.0 * math.pi / (4 * n_ctx * tok_len))
    turns = np.stack([np.cos(turn), -np.sin(turn)])
    inner = (lags[:, None] * lags[None, :] % tok_len) * (2.0 * math.pi / tok_len)
    waves = np.concatenate([np.cos(inner), np.sin(inner)], axis=0)
    return (
        over_blocks.astype(np.float32),
        spread.astype(np.float32).astype(jnp.bfloat16),
        turns.astype(np.float32),
        waves.astype(np.float32).astype(jnp.bfloat16),
    )


def dot(a, b, **kw):
    return jnp.dot(a, b, preferred_element_type=F32, **kw)


def kernel(
    n_ctx, n_fft, group_size,
    tok_hbm, w_hbm, taps_hbm, filt_hbm, gain_hbm, wout_hbm, over_hbm, spread_hbm, turns_hbm, waves_hbm,
    kept_out, cross_out,
    tok, w, taps_in, filt, gain_in, wout, over, spread, turns, waves,
    spread_t, proj, mixed, query, send, recv, filt_send, filt_recv,
    signal, lhs, lhs2, spec, back, send2, recv2, gated, part, kept,
    pair_send, pair_recv, cross_send, twin_query, twin_mixed,
    load_sem, rim_send_sem, rim_recv_sem, filt_sem, go_send_sem, go_recv_sem, come_send_sem, come_recv_sem,
    pair_send_sem, pair_recv_sem, cross_send_sem, cross_recv_sem, twin_sem,
):
    me = lax.axis_index("ctx")
    fft = lax.axis_index("fft")
    chip = fft // 2
    core = fft % 2
    twin = me + 1 - 2 * (me % 2)
    partner = chip * 2 + (1 - core)
    across = (1 - chip) * 2 + core
    tok_len, width = tok.shape
    block = w.shape[2]
    stretch = block // n_ctx
    rows = n_ctx * stretch
    n_taps = taps_in.shape[0]
    piece = tok_len // n_fft
    half = tok_len // 2
    tc = min(128, half)
    lc = min(128, block)
    per_lc = lc // stretch

    barrier = pltpu.get_barrier_semaphore()

    def each_peer(act):
        def around(offset):
            peer = me + offset
            return jnp.where(peer >= n_ctx, peer - n_ctx, peer)

        far = n_ctx // 2
        group = next(g for g in (5, 3, 1) if (far - 2) % g == 0)
        act(around(far))
        act(around(far - 1))
        act(around(n_ctx - far + 1))

        if far > 2:
            @pl.loop(0, (far - 2) // group)
            def _(i):
                for j in range(group):
                    d = far - 2 - j - i * group
                    act(around(d))
                    act(around(n_ctx - d))

    split = half - 16
    loads = {}
    for slot, (name, src, dst) in enumerate([
        ("taps", taps_hbm, taps_in),
        ("tok1", tok_hbm.at[pl.ds(split, tok_len - split)], tok.at[pl.ds(split, tok_len - split)]),
        ("w1", w_hbm.at[1], w.at[1]), ("w2", w_hbm.at[2], w.at[2]),
        ("filt", filt_hbm, filt), ("tok0", tok_hbm.at[pl.ds(0, split)], tok.at[pl.ds(0, split)]),
        ("w0", w_hbm.at[0], w.at[0]), ("gain", gain_hbm, gain_in),
        ("spread", spread_hbm, spread), ("over", over_hbm, over), ("turns", turns_hbm, turns),
        ("waves", waves_hbm, waves), ("wout", wout_hbm, wout),
    ]):
        loads[name] = pltpu.make_async_copy(src, dst, load_sem.at[slot])
        loads[name].start()
        if name == "w2":
            each_peer(lambda peer: pl.semaphore_signal(barrier, inc=1, device_id={"ctx": peer}, device_id_type=MESH))
            for other in (partner, across, (1 - chip) * 2 + (1 - core)):
                pl.semaphore_signal(barrier, inc=1, device_id={"fft": other}, device_id_type=MESH)
            for k in range(2):
                pl.semaphore_signal(
                    barrier, inc=1, device_id={"ctx": twin, "fft": (1 - chip) * 2 + k}, device_id_type=MESH)

    first_group = fft * (block // group_size)
    per_stream = taps_in.shape[1] // 3
    loads["taps"].wait()
    group_of = lax.broadcasted_iota(jnp.int32, (per_stream, block), 1) // group_size + first_group
    pick = (lax.broadcasted_iota(jnp.int32, (per_stream, block), 0) == group_of).astype(F32)
    blank = jnp.zeros((8 - n_taps, per_stream), F32)
    taps_rows = jnp.concatenate(
        [x for s in range(3) for x in (taps_in[:, s * per_stream:(s + 1) * per_stream], blank)], axis=0
    )
    taps_all = dot(taps_rows, pick, precision=lax.Precision.HIGHEST)

    def project(s, r0, r1):
        for n0 in range(0, block, min(256, block)):
            n1 = n0 + min(256, block)
            got = dot(tok[r0:r1, :], w[s, :, n0:n1])
            got = got.astype(BF16).astype(F32)
            for c0 in range(n0, n1, lc):
                proj[s, c0 // lc, RIM + r0:RIM + r1, :] = got[:, c0 - n0:c0 - n0 + lc]

    def rim_copy(s):
        return pltpu.make_async_remote_copy(
            src_ref=proj.at[s, :, pl.ds(tok_len, RIM), :], dst_ref=proj.at[s, :, pl.ds(0, RIM), :],
            send_sem=rim_send_sem.at[s], recv_sem=rim_recv_sem.at[s],
            device_id={"ctx": lax.rem(me + 1, n_ctx)}, device_id_type=MESH,
        )

    def send_rim(s):
        @pl.when(me < n_ctx - 1)
        def _():
            rim_copy(s).start()

        @pl.when(me == 0)
        def _():
            proj[s, :, 0:RIM, :] = jnp.zeros((block // lc, RIM, lc), F32)

    def finish_rim(s):
        @pl.when(me > 0)
        def _():
            rim_copy(s).wait_recv()

    def featurize(s, t0, c0):
        total = None
        for j in range(n_taps):
            term = taps_all[s * 8 + j:s * 8 + j + 1, c0:c0 + lc] * proj[s, c0 // lc, pl.ds(t0 + (RIM - j), tc), :]
            total = term if total is None else total + term
        return total.astype(BF16).astype(F32)

    def mix(t0, c0):
        both = featurize(1, t0, c0) * featurize(2, t0, c0)
        mixed[pl.ds(t0, tc), c0:c0 + lc] = both
        turned = both.T.reshape(per_lc, stretch, tc).astype(BF16)
        send[c0 // stretch:c0 // stretch + per_lc, :, pl.ds(t0, tc)] = turned

    def exchange(source, target, send_sem, recv_sem):
        def held_for(dest, crossed):
            return dest + 1 - 2 * (dest % 2) if crossed else dest

        def copy_to(dest, h0, size, i, crossed):
            return pltpu.make_async_remote_copy(
                src_ref=source.at[held_for(dest, crossed), :, pl.ds(h0, size)],
                dst_ref=target.at[me, :, pl.ds(h0, size)],
                send_sem=send_sem.at[i], recv_sem=recv_sem.at[i],
                device_id={"ctx": dest}, device_id_type=MESH,
            )

        def start(h0, size, i, crossed=False):
            each_peer(lambda dest: copy_to(dest, h0, size, i, crossed).start())
            target[me, :, pl.ds(h0, size)] = source[held_for(me, crossed), :, pl.ds(h0, size)]

        def all_of(h0, size, i):
            return pltpu.make_async_remote_copy(
                src_ref=source.at[pl.ds(0, n_ctx - 1), :, pl.ds(h0, size)],
                dst_ref=target.at[pl.ds(0, n_ctx - 1), :, pl.ds(h0, size)],
                send_sem=send_sem.at[i], recv_sem=recv_sem.at[i],
                device_id={"ctx": lax.rem(me + 1, n_ctx)}, device_id_type=MESH,
            )

        return start, all_of

    go_start, go_all = exchange(send, recv, go_send_sem, go_recv_sem)

    loads["tok1"].wait()
    for s, name in ((1, "w1"), (2, "w2")):
        loads[name].wait()
        project(s, split, tok_len)
    for c0 in range(0, block, lc):
        @pl.loop(half // tc, tok_len // tc)
        def _(t):
            mix(pl.multiple_of(t * tc, tc), c0)

    pl.semaphore_wait(barrier, n_ctx - 1 + 3 + 2)
    send_rim(1)
    send_rim(2)
    go_start(half, half, 1)

    loads["filt"].wait()
    flipped = filt[...].T.astype(BF16).astype(F32)
    lag_rows, lag_lanes = filt_send.shape[1:]
    for j in range(lag_rows):
        filt_send[:, j, :] = flipped[:, j * lag_lanes:(j + 1) * lag_lanes].astype(BF16)

    def filt_copy(dest):
        return pltpu.make_async_remote_copy(
            src_ref=filt_send.at[first_group + (dest * stretch) // group_size],
            dst_ref=filt_recv.at[me],
            send_sem=filt_sem.at[0], recv_sem=filt_sem.at[1],
            device_id={"ctx": dest}, device_id_type=MESH,
        )

    filt_all = pltpu.make_async_remote_copy(
        src_ref=filt_recv.at[pl.ds(0, n_ctx - 1)], dst_ref=filt_recv.at[pl.ds(0, n_ctx - 1)],
        send_sem=filt_sem.at[0], recv_sem=filt_sem.at[1],
        device_id={"ctx": lax.rem(me + 1, n_ctx)}, device_id_type=MESH,
    )
    filt_recv[me] = filt_send[first_group + (me * stretch) // group_size]
    each_peer(lambda dest: filt_copy(dest).start())

    loads["tok0"].wait()
    project(1, 0, split)
    project(2, 0, split)
    for c0 in range(0, block, lc):
        @pl.loop(1, half // tc)
        def _(t):
            mix(pl.multiple_of(t * tc, tc), c0)

    finish_rim(1)
    finish_rim(2)
    for c0 in range(0, block, lc):
        mix(0, c0)
    go_start(0, half, 0)

    loads["w0"].wait()
    project(0, 0, tok_len)
    send_rim(0)
    loads["spread"].wait()
    spread_t[...] = spread[...].T

    kc = min(8, n_ctx)
    kr = kc * stretch
    mc = min(256, rows)

    def turned_by(table, re, im, m0, cols):
        n = re.shape[1]
        re = re.reshape(-1, stretch, n)
        im = im.reshape(-1, stretch, n)
        k0 = m0 // stretch
        b_re = table[0, k0:k0 + re.shape[0], cols][:, None, :]
        b_im = table[1, k0:k0 + re.shape[0], cols][:, None, :]
        return re, im, b_re, b_im

    loads["turns"].wait()

    def first_stage(h0):
        @pl.loop(0, n_ctx // kc)
        def _(i):
            got = recv[pl.ds(i * kc, kc), :, h0:h0 + half].astype(F32)
            signal[pl.ds(pl.multiple_of(i * kr, kr), kr), h0:h0 + half] = got.reshape(kr, half).astype(BF16)

        for m0 in range(0, rows, mc):
            re, im, b_re, b_im = turned_by(
                turns, dot(spread[m0:m0 + mc, :], signal[:, h0:h0 + half]),
                dot(spread[rows + m0:rows + m0 + mc, :], signal[:, h0:h0 + half]), m0, pl.ds(h0, half))
            o_re = (re * b_re - im * b_im).reshape(mc, half)
            o_im = (re * b_im + im * b_re).reshape(mc, half)
            lhs[m0:m0 + mc, h0:h0 + half] = o_re.astype(BF16)
            lhs[m0:m0 + mc, tok_len + h0:tok_len + h0 + half] = o_im.astype(BF16)
            lhs[rows + m0:rows + m0 + mc, h0:h0 + half] = o_im.astype(BF16)
            lhs[rows + m0:rows + m0 + mc, tok_len + h0:tok_len + h0 + half] = (-o_re).astype(BF16)

    loads["over"].wait()
    loads["waves"].wait()
    filt_all.wait_recv()
    lags3 = filt_recv[...].astype(F32)
    lags = jnp.concatenate([lags3[:, j, :] for j in range(lag_rows)], axis=1).astype(BF16)
    first = dot(over[...].astype(BF16), lags)
    f_re, f_im = first[:n_ctx], first[n_ctx:]
    t_re, t_im = turns[0], turns[1]
    g_re = (f_re * t_re - f_im * t_im).astype(BF16)
    g_im = (f_re * t_im + f_im * t_re).astype(BF16)
    top = jnp.concatenate([g_re, g_im], axis=1)
    bottom = jnp.concatenate([g_im, -g_re], axis=1)
    scale = 1.0 / (n_ctx * tok_len)
    spec[0] = dot(top, waves[...]) * scale
    spec[1] = dot(bottom, waves[...]) * scale

    go_all(half, half, 1).wait_recv()
    first_stage(half)

    finish_rim(0)
    for c0 in range(0, block, lc):
        @pl.loop(0, tok_len // tc)
        def _(t):
            t0 = pl.multiple_of(t * tc, tc)
            query[pl.ds(t0, tc), c0:c0 + lc] = featurize(0, t0, c0).astype(BF16)

    theirs = (1 - chip) * half
    ours = pl.multiple_of(chip * half, half)
    parts = [pl.multiple_of(theirs + j * piece, piece) for j in range(2)]
    twin_mixed[0] = mixed[pl.ds(parts[1], piece), :].astype(BF16)

    def twin_copy(i):
        return pltpu.make_async_remote_copy(
            src_ref=(query.at[pl.ds(parts[1], piece)], twin_mixed.at[0])[i],
            dst_ref=(twin_query, twin_mixed.at[1])[i],
            send_sem=twin_sem.at[0, i], recv_sem=twin_sem.at[1, i],
            device_id={"ctx": twin}, device_id_type=MESH,
        )

    twin_copy(0).start()
    twin_copy(1).start()

    go_all(0, half, 0).wait_recv()
    first_stage(0)

    for m0 in range(0, rows, mc):
        re, im, b_re, b_im = turned_by(
            spec, dot(lhs[m0:m0 + mc, :], waves[...]), dot(lhs[rows + m0:rows + m0 + mc, :], waves[...]),
            m0, slice(None))
        o_re = (re * b_re - im * b_im).reshape(mc, tok_len)
        o_im = (re * b_im + im * b_re).reshape(mc, tok_len)
        lhs2[m0:m0 + mc, :tok_len] = o_re.astype(BF16)
        lhs2[m0:m0 + mc, tok_len:] = (-o_im).astype(BF16)
        lhs2[rows + m0:rows + m0 + mc, :tok_len] = o_im.astype(BF16)
        lhs2[rows + m0:rows + m0 + mc, tok_len:] = o_re.astype(BF16)

    come_start, come_all = exchange(send2, recv2, come_send_sem, come_recv_sem)

    def last_stage(h0, size):
        cols = pl.ds(h0, size)
        for m0 in range(0, rows, mc):
            re, im, b_re, b_im = turned_by(
                turns, dot(lhs2[m0:m0 + mc, :], waves[:, cols]),
                dot(lhs2[rows + m0:rows + m0 + mc, :], waves[:, cols]), m0, cols)
            back[m0:m0 + mc, :size] = (re * b_re + im * b_im).reshape(mc, size).astype(BF16)
            back[rows + m0:rows + m0 + mc, :size] = (im * b_re - re * b_im).reshape(mc, size).astype(BF16)

        for m0 in range(0, rows, mc):
            got = dot(spread_t[m0:m0 + mc, :], back[:, :size])
            send2[m0 // stretch:(m0 + mc) // stretch, :, cols] = (
                got.reshape(mc // stretch, stretch, size).astype(BF16))

    for j in range(2):
        last_stage(parts[j], piece)
        come_start(parts[j], piece, j, crossed=j == 1)
    last_stage(ours, half)
    come_start(ours, half, 2)

    loads["wout"].wait()
    loads["gain"].wait()
    gain_row = gain_in[:, pl.ds(pl.multiple_of(fft * block, block), block)]
    n_chunks, oc = part.shape[0], part.shape[2]
    share = n_chunks // 2
    gc = min(128, piece)

    def gate(h0, size, asked, direct, off):
        for c0 in range(0, block, lc):
            for t in range(0, size, gc):
                t0 = pl.multiple_of(h0 + t, gc)
                got = recv2[c0 // stretch:c0 // stretch + per_lc, :, pl.ds(t0, gc)].astype(F32)
                conv = got.reshape(lc, gc).T
                at = pl.multiple_of(off + t, gc)
                whole = conv + gain_row[:, c0:c0 + lc] * direct[pl.ds(at, gc), c0:c0 + lc].astype(F32)
                gated[pl.ds(t0, gc), c0:c0 + lc] = (
                    asked[pl.ds(at, gc), c0:c0 + lc].astype(F32) * whole).astype(BF16)

    def pair_copy(n):
        return pltpu.make_async_remote_copy(
            src_ref=pair_send.at[n], dst_ref=pair_recv.at[n],
            send_sem=pair_send_sem.at[n], recv_sem=pair_recv_sem.at[n],
            device_id={"fft": partner}, device_id_type=MESH,
        )

    def cross_copy(j, i):
        n = core * share + i
        return pltpu.make_async_remote_copy(
            src_ref=cross_send.at[j, i], dst_ref=cross_out.at[:, pl.ds(pl.multiple_of(n * oc, oc), oc)],
            send_sem=cross_send_sem.at[j, i], recv_sem=cross_recv_sem.at[n],
            device_id={"ctx": twin if j else me, "fft": (1 - chip) * 2 + j}, device_id_type=MESH,
        )

    def cross_arrival(n):
        return pltpu.make_async_remote_copy(
            src_ref=cross_send.at[0, 0], dst_ref=cross_out.at[:, n * oc:(n + 1) * oc],
            send_sem=cross_send_sem.at[0, 0], recv_sem=cross_recv_sem.at[n],
            device_id={"fft": across}, device_id_type=MESH,
        )

    def product(h0, size, n):
        return dot(gated[pl.ds(h0, size), :], wout[:, pl.ds(pl.multiple_of(n * oc, oc), oc)])

    go_all(half, half, 1).wait_send()
    go_all(0, half, 0).wait_send()
    filt_all.wait_send()

    @pl.when(me < n_ctx - 1)
    def _():
        for s in range(3):
            rim_copy(s).wait_send()

    for j in range(2):
        come_all(parts[j], piece, j).wait_recv()
        if j == 0:
            gate(parts[j], piece, query, mixed, parts[j])
        else:
            twin_copy(0).wait_recv()
            twin_copy(1).wait_recv()
            gate(parts[j], piece, twin_query, twin_mixed.at[1], 0)
        for i in range(share):
            pair_send[j * share + i] = product(parts[j], piece, (1 - core) * share + i).astype(BF16)
            pair_copy(j * share + i).start()
        for i in range(share):
            part[i, j * piece:(j + 1) * piece, :] = product(parts[j], piece, core * share + i)
    for j in range(2):
        for i in range(share):
            pair_copy(j * share + i).wait_recv()
            mine = part[i, j * piece:(j + 1) * piece, :]
            cross_send[j, i] = (mine + pair_recv[j * share + i].astype(F32)).astype(BF16)
            cross_copy(j, i).start()

    come_all(ours, half, 2).wait_recv()
    gate(ours, half, query, mixed, ours)
    for n in range(n_chunks):
        part[n] = product(ours, half, n)
        other = part[n, pl.ds(pl.multiple_of((1 - core) * piece, piece), piece), :]
        pair_send[n_chunks + n] = other.astype(BF16)
        pair_copy(n_chunks + n).start()
    for n in range(n_chunks):
        pair_copy(n_chunks + n).wait_recv()
        mine = part[n, pl.ds(pl.multiple_of(core * piece, piece), piece), :]
        kept[:, n * oc:(n + 1) * oc] = (mine + pair_recv[n_chunks + n].astype(F32)).astype(BF16)
    keep = pltpu.make_async_copy(kept, kept_out, load_sem.at[0])
    keep.start()

    come_all(parts[0], piece, 0).wait_send()
    come_all(parts[1], piece, 1).wait_send()
    come_all(ours, half, 2).wait_send()
    for n in range(2 * n_chunks):
        pair_copy(n).wait_send()
    keep.wait()
    twin_copy(0).wait_send()
    twin_copy(1).wait_send()
    for n in range(n_chunks):
        cross_arrival(n).wait_recv()
    for j in range(2):
        for i in range(share):
            cross_copy(j, i).wait_send()


def body(tokens, w_in, short_taps, long_filter, skip_gain, w_out):
    n_ctx = lax.axis_size("ctx")
    n_fft = lax.axis_size("fft")
    tok_len, width = tokens.shape
    block = w_in.shape[2]
    n_groups = long_filter.shape[1]
    group_size = width // n_groups
    stretch = block // n_ctx
    rows = n_ctx * stretch
    piece = tok_len // n_fft
    oc = min(512, width // 4)
    n_chunks = width // oc
    lag_rows = 4
    lc = min(128, block)
    over, spread, turns, waves = tables(n_ctx, tok_len, stretch)
    dma = pltpu.SemaphoreType.DMA
    vmem = pltpu.VMEM
    streams = w_in.transpose(1, 0, 2)
    args = (
        tokens, streams, short_taps, long_filter, skip_gain.reshape(1, width), w_out,
        jnp.asarray(over), jnp.asarray(spread), jnp.asarray(turns), jnp.asarray(waves),
    )
    kept, crossed = pl.pallas_call(
        functools.partial(kernel, n_ctx, n_fft, group_size),
        out_shape=(jax.ShapeDtypeStruct((piece, width), BF16), jax.ShapeDtypeStruct((piece, width), BF16)),
        in_specs=[pl.BlockSpec(memory_space=pl.ANY)] * len(args),
        out_specs=(pl.BlockSpec(memory_space=pl.ANY), pl.BlockSpec(memory_space=pl.ANY)),
        scratch_shapes=[vmem(a.shape, a.dtype) for a in args] + [
            vmem((rows, 2 * rows), BF16),
            vmem((3, block // lc, tok_len + RIM, lc), F32),
            vmem((tok_len, block), F32),
            vmem((tok_len, block), BF16),
            vmem((n_ctx, stretch, tok_len), BF16),
            vmem((n_ctx, stretch, tok_len), BF16),
            vmem((n_groups, lag_rows, tok_len // lag_rows), BF16),
            vmem((n_ctx, lag_rows, tok_len // lag_rows), BF16),
            vmem((rows, tok_len), BF16),
            vmem((2 * rows, 2 * tok_len), BF16),
            vmem((2 * rows, 2 * tok_len), BF16),
            vmem((2, n_ctx, tok_len), F32),
            vmem((2 * rows, tok_len // 2), BF16),
            vmem((n_ctx, stretch, tok_len), BF16),
            vmem((n_ctx, stretch, tok_len), BF16),
            vmem((tok_len, block), BF16),
            vmem((n_chunks, tok_len // 2, oc), F32),
            vmem((piece, width), BF16),
            vmem((2 * n_chunks, piece, oc), BF16),
            vmem((2 * n_chunks, piece, oc), BF16),
            vmem((2, n_chunks // 2, piece, oc), BF16),
            vmem((piece, block), BF16),
            vmem((2, piece, block), BF16),
            dma((13,)), dma((3,)), dma((3,)), dma((2,)), dma((2,)), dma((2,)), dma((3,)), dma((3,)),
            dma((2 * n_chunks,)), dma((2 * n_chunks,)), dma((2, n_chunks // 2)), dma((n_chunks,)), dma((2, 2)),
        ],
        compiler_params=pltpu.CompilerParams(
            collective_id=0, has_side_effects=True, vmem_limit_bytes=60 * 1024 * 1024
        ),
        name="hyena",
    )(*args)
    return (kept.astype(F32) + crossed.astype(F32)).astype(BF16)


def solution(mesh):
    return jax.shard_map(
        body,
        mesh=mesh,
        in_specs=(P("ctx", None), P(None, None, "fft"), P(), P("ctx", None), P(), P("fft", None)),
        out_specs=P(("ctx", "fft"), None),
        check_vma=False,
    )
```

```python
import functools
import math

import jax
import jax.numpy as jnp
import numpy as np
from jax import lax
from jax.experimental import pallas as pl
from jax.experimental.pallas import tpu as pltpu
from jax.sharding import PartitionSpec as P

MESH = pl.DeviceIdType.MESH
F32 = jnp.float32
BF16 = jnp.bfloat16
RIM = 8


def tables(n_ctx, tok_len, stretch):
    blocks = np.arange(n_ctx)
    lags = np.arange(tok_len)
    odd = 2 * blocks + 1
    angle = (odd[:, None] * blocks[None, :] % (4 * n_ctx)) * (2.0 * math.pi / (4 * n_ctx))
    eye = np.eye(stretch)
    over_blocks = np.concatenate([np.cos(angle), -np.sin(angle)], axis=0)
    spread = np.kron(over_blocks, eye)
    turn = (odd[:, None] * lags[None, :]) * (2.0 * math.pi / (4 * n_ctx * tok_len))
    turns = np.stack([np.cos(turn), -np.sin(turn)])
    inner = (lags[:, None] * lags[None, :] % tok_len) * (2.0 * math.pi / tok_len)
    waves = np.concatenate([np.cos(inner), np.sin(inner)], axis=0)
    return (
        over_blocks.astype(np.float32),
        spread.astype(np.float32).astype(jnp.bfloat16),
        turns.astype(np.float32),
        waves.astype(np.float32).astype(jnp.bfloat16),
    )


def dot(a, b, **kw):
    return jnp.dot(a, b, preferred_element_type=F32, **kw)


def kernel(
    n_ctx, n_fft, group_size,
    tok_hbm, w_hbm, taps_hbm, filt_hbm, gain_hbm, wout_hbm, over_hbm, spread_hbm, turns_hbm, waves_hbm,
    kept_out, cross_out,
    tok, w, taps_in, filt, gain_in, wout, over, spread, turns, waves,
    spread_t, proj, mixed, query, send, recv, filt_send, filt_recv,
    signal, lhs, lhs2, spec, back, send2, recv2, gated, part, kept,
    pair_send, pair_recv, cross_send, twin_query, twin_mixed,
    load_sem, rim_send_sem, rim_recv_sem, filt_sem, go_send_sem, go_recv_sem, come_send_sem, come_recv_sem,
    pair_send_sem, pair_recv_sem, cross_send_sem, cross_recv_sem, twin_sem,
):
    me = lax.axis_index("ctx")
    fft = lax.axis_index("fft")
    chip = fft // 2
    core = fft % 2
    twin = me + 1 - 2 * (me % 2)
    partner = chip * 2 + (1 - core)
    across = (1 - chip) * 2 + core
    tok_len, width = tok.shape
    block = w.shape[2]
    stretch = block // n_ctx
    rows = n_ctx * stretch
    n_taps = taps_in.shape[0]
    piece = tok_len // n_fft
    half = tok_len // 2
    tc = min(128, half)
    lc = min(128, block)
    per_lc = lc // stretch

    barrier = pltpu.get_barrier_semaphore()

    def each_peer(act):
        def around(offset):
            peer = me + offset
            return jnp.where(peer >= n_ctx, peer - n_ctx, peer)

        far = n_ctx // 2
        group = next(g for g in (5, 3, 1) if (far - 2) % g == 0)
        act(around(far))
        act(around(far - 1))
        act(around(n_ctx - far + 1))

        if far > 2:
            @pl.loop(0, (far - 2) // group)
            def _(i):
                for j in range(group):
                    d = far - 2 - j - i * group
                    act(around(d))
                    act(around(n_ctx - d))

    split = half - 16
    loads = {}
    for slot, (name, src, dst) in enumerate([
        ("taps", taps_hbm, taps_in),
        ("tok1", tok_hbm.at[pl.ds(split, tok_len - split)], tok.at[pl.ds(split, tok_len - split)]),
        ("w1", w_hbm.at[1], w.at[1]), ("w2", w_hbm.at[2], w.at[2]),
        ("filt", filt_hbm, filt), ("tok0", tok_hbm.at[pl.ds(0, split)], tok.at[pl.ds(0, split)]),
        ("w0", w_hbm.at[0], w.at[0]), ("gain", gain_hbm, gain_in),
        ("spread", spread_hbm, spread), ("over", over_hbm, over), ("turns", turns_hbm, turns),
        ("waves", waves_hbm, waves), ("wout", wout_hbm, wout),
    ]):
        loads[name] = pltpu.make_async_copy(src, dst, load_sem.at[slot])
        loads[name].start()
        if name == "w2":
            each_peer(lambda peer: pl.semaphore_signal(barrier, inc=1, device_id={"ctx": peer}, device_id_type=MESH))
            for other in (partner, across, (1 - chip) * 2 + (1 - core)):
                pl.semaphore_signal(barrier, inc=1, device_id={"fft": other}, device_id_type=MESH)
            for k in range(2):
                pl.semaphore_signal(
                    barrier, inc=1, device_id={"ctx": twin, "fft": (1 - chip) * 2 + k}, device_id_type=MESH)

    first_group = fft * (block // group_size)
    per_stream = taps_in.shape[1] // 3
    loads["taps"].wait()
    group_of = lax.broadcasted_iota(jnp.int32, (per_stream, block), 1) // group_size + first_group
    pick = (lax.broadcasted_iota(jnp.int32, (per_stream, block), 0) == group_of).astype(F32)
    blank = jnp.zeros((8 - n_taps, per_stream), F32)
    taps_rows = jnp.concatenate(
        [x for s in range(3) for x in (taps_in[:, s * per_stream:(s + 1) * per_stream], blank)], axis=0
    )
    taps_all = dot(taps_rows, pick, precision=lax.Precision.HIGHEST)

    def project(s, r0, r1):
        for n0 in range(0, block, min(256, block)):
            n1 = n0 + min(256, block)
            got = dot(tok[r0:r1, :], w[s, :, n0:n1])
            got = got.astype(BF16).astype(F32)
            for c0 in range(n0, n1, lc):
                proj[s, c0 // lc, RIM + r0:RIM + r1, :] = got[:, c0 - n0:c0 - n0 + lc]

    def rim_copy(s):
        return pltpu.make_async_remote_copy(
            src_ref=proj.at[s, :, pl.ds(tok_len, RIM), :], dst_ref=proj.at[s, :, pl.ds(0, RIM), :],
            send_sem=rim_send_sem.at[s], recv_sem=rim_recv_sem.at[s],
            device_id={"ctx": lax.rem(me + 1, n_ctx)}, device_id_type=MESH,
        )

    def send_rim(s):
        @pl.when(me < n_ctx - 1)
        def _():
            rim_copy(s).start()

        @pl.when(me == 0)
        def _():
            proj[s, :, 0:RIM, :] = jnp.zeros((block // lc, RIM, lc), F32)

    def finish_rim(s):
        @pl.when(me > 0)
        def _():
            rim_copy(s).wait_recv()

    def featurize(s, t0, c0):
        total = None
        for j in range(n_taps):
            term = taps_all[s * 8 + j:s * 8 + j + 1, c0:c0 + lc] * proj[s, c0 // lc, pl.ds(t0 + (RIM - j), tc), :]
            total = term if total is None else total + term
        return total.astype(BF16).astype(F32)

    def keys(t0, c0):
        mixed[pl.ds(t0, tc), c0:c0 + lc] = featurize(1, t0, c0)

    def mix(t0, c0):
        both = mixed[pl.ds(t0, tc), c0:c0 + lc] * featurize(2, t0, c0)
        mixed[pl.ds(t0, tc), c0:c0 + lc] = both
        turned = both.T.reshape(per_lc, stretch, tc).astype(BF16)
        send[c0 // stretch:c0 // stretch + per_lc, :, pl.ds(t0, tc)] = turned

    def exchange(source, target, send_sem, recv_sem):
        def held_for(dest, crossed):
            return dest + 1 - 2 * (dest % 2) if crossed else dest

        def copy_to(dest, h0, size, i, crossed):
            return pltpu.make_async_remote_copy(
                src_ref=source.at[held_for(dest, crossed), :, pl.ds(h0, size)],
                dst_ref=target.at[me, :, pl.ds(h0, size)],
                send_sem=send_sem.at[i], recv_sem=recv_sem.at[i],
                device_id={"ctx": dest}, device_id_type=MESH,
            )

        def start(h0, size, i, crossed=False):
            each_peer(lambda dest: copy_to(dest, h0, size, i, crossed).start())
            target[me, :, pl.ds(h0, size)] = source[held_for(me, crossed), :, pl.ds(h0, size)]

        def all_of(h0, size, i):
            return pltpu.make_async_remote_copy(
                src_ref=source.at[pl.ds(0, n_ctx - 1), :, pl.ds(h0, size)],
                dst_ref=target.at[pl.ds(0, n_ctx - 1), :, pl.ds(h0, size)],
                send_sem=send_sem.at[i], recv_sem=recv_sem.at[i],
                device_id={"ctx": lax.rem(me + 1, n_ctx)}, device_id_type=MESH,
            )

        return start, all_of

    go_start, go_all = exchange(send, recv, go_send_sem, go_recv_sem)

    loads["tok1"].wait()
    for s, name in ((1, "w1"), (2, "w2")):
        loads[name].wait()
        project(s, split, tok_len)
        for c0 in range(0, block, lc):
            @pl.loop(half // tc, tok_len // tc)
            def _(t):
                (keys if s == 1 else mix)(pl.multiple_of(t * tc, tc), c0)

    pl.semaphore_wait(barrier, n_ctx - 1 + 3 + 2)
    send_rim(1)
    send_rim(2)
    go_start(half, half, 1)

    loads["filt"].wait()
    flipped = filt[...].T.astype(BF16).astype(F32)
    lag_rows, lag_lanes = filt_send.shape[1:]
    for j in range(lag_rows):
        filt_send[:, j, :] = flipped[:, j * lag_lanes:(j + 1) * lag_lanes].astype(BF16)

    def filt_copy(dest):
        return pltpu.make_async_remote_copy(
            src_ref=filt_send.at[first_group + (dest * stretch) // group_size],
            dst_ref=filt_recv.at[me],
            send_sem=filt_sem.at[0], recv_sem=filt_sem.at[1],
            device_id={"ctx": dest}, device_id_type=MESH,
        )

    filt_all = pltpu.make_async_remote_copy(
        src_ref=filt_recv.at[pl.ds(0, n_ctx - 1)], dst_ref=filt_recv.at[pl.ds(0, n_ctx - 1)],
        send_sem=filt_sem.at[0], recv_sem=filt_sem.at[1],
        device_id={"ctx": lax.rem(me + 1, n_ctx)}, device_id_type=MESH,
    )
    filt_recv[me] = filt_send[first_group + (me * stretch) // group_size]
    each_peer(lambda dest: filt_copy(dest).start())

    loads["tok0"].wait()
    project(1, 0, split)
    project(2, 0, split)
    for c0 in range(0, block, lc):
        @pl.loop(1, half // tc)
        def _(t):
            keys(pl.multiple_of(t * tc, tc), c0)
            mix(pl.multiple_of(t * tc, tc), c0)

    finish_rim(1)
    finish_rim(2)
    for c0 in range(0, block, lc):
        keys(0, c0)
        mix(0, c0)
    go_start(0, half, 0)

    loads["w0"].wait()
    project(0, 0, tok_len)
    send_rim(0)
    loads["spread"].wait()
    spread_t[...] = spread[...].T

    kc = min(8, n_ctx)
    kr = kc * stretch
    mc = min(256, rows)

    def turned_by(table, re, im, m0, cols):
        n = re.shape[1]
        re = re.reshape(-1, stretch, n)
        im = im.reshape(-1, stretch, n)
        k0 = m0 // stretch
        b_re = table[0, k0:k0 + re.shape[0], cols][:, None, :]
        b_im = table[1, k0:k0 + re.shape[0], cols][:, None, :]
        return re, im, b_re, b_im

    loads["turns"].wait()

    def first_stage(h0):
        @pl.loop(0, n_ctx // kc)
        def _(i):
            got = recv[pl.ds(i * kc, kc), :, h0:h0 + half].astype(F32)
            signal[pl.ds(pl.multiple_of(i * kr, kr), kr), h0:h0 + half] = got.reshape(kr, half).astype(BF16)

        for m0 in range(0, rows, mc):
            re, im, b_re, b_im = turned_by(
                turns, dot(spread[m0:m0 + mc, :], signal[:, h0:h0 + half]),
                dot(spread[rows + m0:rows + m0 + mc, :], signal[:, h0:h0 + half]), m0, pl.ds(h0, half))
            o_re = (re * b_re - im * b_im).reshape(mc, half)
            o_im = (re * b_im + im * b_re).reshape(mc, half)
            lhs[m0:m0 + mc, h0:h0 + half] = o_re.astype(BF16)
            lhs[m0:m0 + mc, tok_len + h0:tok_len + h0 + half] = o_im.astype(BF16)
            lhs[rows + m0:rows + m0 + mc, h0:h0 + half] = o_im.astype(BF16)
            lhs[rows + m0:rows + m0 + mc, tok_len + h0:tok_len + h0 + half] = (-o_re).astype(BF16)

    loads["over"].wait()
    loads["waves"].wait()
    filt_all.wait_recv()
    lags3 = filt_recv[...].astype(F32)
    lags = jnp.concatenate([lags3[:, j, :] for j in range(lag_rows)], axis=1).astype(BF16)
    first = dot(over[...].astype(BF16), lags)
    f_re, f_im = first[:n_ctx], first[n_ctx:]
    t_re, t_im = turns[0], turns[1]
    g_re = (f_re * t_re - f_im * t_im).astype(BF16)
    g_im = (f_re * t_im + f_im * t_re).astype(BF16)
    top = jnp.concatenate([g_re, g_im], axis=1)
    bottom = jnp.concatenate([g_im, -g_re], axis=1)
    scale = 1.0 / (n_ctx * tok_len)
    spec[0] = dot(top, waves[...]) * scale
    spec[1] = dot(bottom, waves[...]) * scale

    go_all(half, half, 1).wait_recv()
    first_stage(half)

    theirs = (1 - chip) * half
    ours = pl.multiple_of(chip * half, half)
    parts = [pl.multiple_of(theirs + j * piece, piece) for j in range(2)]
    twin_mixed[0] = mixed[pl.ds(parts[1], piece), :].astype(BF16)

    def twin_copy(i):
        return pltpu.make_async_remote_copy(
            src_ref=(query.at[pl.ds(parts[1], piece)], twin_mixed.at[0])[i],
            dst_ref=(twin_query, twin_mixed.at[1])[i],
            send_sem=twin_sem.at[0, i], recv_sem=twin_sem.at[1, i],
            device_id={"ctx": twin}, device_id_type=MESH,
        )

    twin_copy(1).start()

    go_all(0, half, 0).wait_recv()
    first_stage(0)

    for m0 in range(0, rows, mc):
        re, im, b_re, b_im = turned_by(
            spec, dot(lhs[m0:m0 + mc, :], waves[...]), dot(lhs[rows + m0:rows + m0 + mc, :], waves[...]),
            m0, slice(None))
        o_re = (re * b_re - im * b_im).reshape(mc, tok_len)
        o_im = (re * b_im + im * b_re).reshape(mc, tok_len)
        lhs2[m0:m0 + mc, :tok_len] = o_re.astype(BF16)
        lhs2[m0:m0 + mc, tok_len:] = (-o_im).astype(BF16)
        lhs2[rows + m0:rows + m0 + mc, :tok_len] = o_im.astype(BF16)
        lhs2[rows + m0:rows + m0 + mc, tok_len:] = o_re.astype(BF16)

    come_start, come_all = exchange(send2, recv2, come_send_sem, come_recv_sem)

    def last_stage(h0, size):
        cols = pl.ds(h0, size)
        for m0 in range(0, rows, mc):
            re, im, b_re, b_im = turned_by(
                turns, dot(lhs2[m0:m0 + mc, :], waves[:, cols]),
                dot(lhs2[rows + m0:rows + m0 + mc, :], waves[:, cols]), m0, cols)
            back[m0:m0 + mc, :size] = (re * b_re + im * b_im).reshape(mc, size).astype(BF16)
            back[rows + m0:rows + m0 + mc, :size] = (im * b_re - re * b_im).reshape(mc, size).astype(BF16)

        for m0 in range(0, rows, mc):
            got = dot(spread_t[m0:m0 + mc, :], back[:, :size])
            send2[m0 // stretch:(m0 + mc) // stretch, :, cols] = (
                got.reshape(mc // stretch, stretch, size).astype(BF16))

    last_stage(pl.multiple_of(theirs, half), half)
    for j in range(2):
        come_start(parts[j], piece, j, crossed=j == 1)
    last_stage(ours, half)
    finish_rim(0)
    for c0 in range(0, block, lc):
        @pl.loop(0, tok_len // tc)
        def _(t):
            t0 = pl.multiple_of(t * tc, tc)
            query[pl.ds(t0, tc), c0:c0 + lc] = featurize(0, t0, c0).astype(BF16)
    twin_copy(0).start()
    come_start(ours, half, 2)

    loads["wout"].wait()
    loads["gain"].wait()
    gain_row = gain_in[:, pl.ds(pl.multiple_of(fft * block, block), block)]
    n_chunks, oc = part.shape[0], part.shape[2]
    share = n_chunks // 2
    gc = min(128, piece)

    def gate(h0, size, asked, direct, off):
        for c0 in range(0, block, lc):
            for t in range(0, size, gc):
                t0 = pl.multiple_of(h0 + t, gc)
                got = recv2[c0 // stretch:c0 // stretch + per_lc, :, pl.ds(t0, gc)].astype(F32)
                conv = got.reshape(lc, gc).T
                at = pl.multiple_of(off + t, gc)
                whole = conv + gain_row[:, c0:c0 + lc] * direct[pl.ds(at, gc), c0:c0 + lc].astype(F32)
                gated[pl.ds(t0, gc), c0:c0 + lc] = (
                    asked[pl.ds(at, gc), c0:c0 + lc].astype(F32) * whole).astype(BF16)

    def pair_copy(n):
        return pltpu.make_async_remote_copy(
            src_ref=pair_send.at[n], dst_ref=pair_recv.at[n],
            send_sem=pair_send_sem.at[n], recv_sem=pair_recv_sem.at[n],
            device_id={"fft": partner}, device_id_type=MESH,
        )

    def cross_copy(j, i):
        n = core * share + i
        return pltpu.make_async_remote_copy(
            src_ref=cross_send.at[j, i], dst_ref=cross_out.at[:, pl.ds(pl.multiple_of(n * oc, oc), oc)],
            send_sem=cross_send_sem.at[j, i], recv_sem=cross_recv_sem.at[n],
            device_id={"ctx": twin if j else me, "fft": (1 - chip) * 2 + j}, device_id_type=MESH,
        )

    def cross_arrival(n):
        return pltpu.make_async_remote_copy(
            src_ref=cross_send.at[0, 0], dst_ref=cross_out.at[:, n * oc:(n + 1) * oc],
            send_sem=cross_send_sem.at[0, 0], recv_sem=cross_recv_sem.at[n],
            device_id={"fft": across}, device_id_type=MESH,
        )

    def product(h0, size, n):
        return dot(gated[pl.ds(h0, size), :], wout[:, pl.ds(pl.multiple_of(n * oc, oc), oc)])

    go_all(half, half, 1).wait_send()
    go_all(0, half, 0).wait_send()
    filt_all.wait_send()

    @pl.when(me < n_ctx - 1)
    def _():
        for s in range(3):
            rim_copy(s).wait_send()

    for j in range(2):
        come_all(parts[j], piece, j).wait_recv()
        if j == 0:
            gate(parts[j], piece, query, mixed, parts[j])
        else:
            twin_copy(0).wait_recv()
            twin_copy(1).wait_recv()
            gate(parts[j], piece, twin_query, twin_mixed.at[1], 0)
        for i in range(share):
            pair_send[j * share + i] = product(parts[j], piece, (1 - core) * share + i).astype(BF16)
            pair_copy(j * share + i).start()
        for i in range(share):
            part[i, j * piece:(j + 1) * piece, :] = product(parts[j], piece, core * share + i)
    for j in range(2):
        for i in range(share):
            pair_copy(j * share + i).wait_recv()
            mine = part[i, j * piece:(j + 1) * piece, :]
            cross_send[j, i] = (mine + pair_recv[j * share + i].astype(F32)).astype(BF16)
            cross_copy(j, i).start()

    come_all(ours, half, 2).wait_recv()
    gate(ours, half, query, mixed, ours)
    for n in range(n_chunks):
        part[n] = product(ours, half, n)
        other = part[n, pl.ds(pl.multiple_of((1 - core) * piece, piece), piece), :]
        pair_send[n_chunks + n] = other.astype(BF16)
        pair_copy(n_chunks + n).start()
    for n in range(n_chunks):
        pair_copy(n_chunks + n).wait_recv()
        mine = part[n, pl.ds(pl.multiple_of(core * piece, piece), piece), :]
        kept[:, n * oc:(n + 1) * oc] = (mine + pair_recv[n_chunks + n].astype(F32)).astype(BF16)
    keep = pltpu.make_async_copy(kept, kept_out, load_sem.at[0])
    keep.start()

    come_all(parts[0], piece, 0).wait_send()
    come_all(parts[1], piece, 1).wait_send()
    come_all(ours, half, 2).wait_send()
    for n in range(2 * n_chunks):
        pair_copy(n).wait_send()
    keep.wait()
    twin_copy(0).wait_send()
    twin_copy(1).wait_send()
    for n in range(n_chunks):
        cross_arrival(n).wait_recv()
    for j in range(2):
        for i in range(share):
            cross_copy(j, i).wait_send()


def body(tokens, w_in, short_taps, long_filter, skip_gain, w_out):
    n_ctx = lax.axis_size("ctx")
    n_fft = lax.axis_size("fft")
    tok_len, width = tokens.shape
    block = w_in.shape[2]
    n_groups = long_filter.shape[1]
    group_size = width // n_groups
    stretch = block // n_ctx
    rows = n_ctx * stretch
    piece = tok_len // n_fft
    oc = min(512, width // 4)
    n_chunks = width // oc
    lag_rows = 4
    lc = min(128, block)
    over, spread, turns, waves = tables(n_ctx, tok_len, stretch)
    dma = pltpu.SemaphoreType.DMA
    vmem = pltpu.VMEM
    streams = w_in.transpose(1, 0, 2)
    args = (
        tokens, streams, short_taps, long_filter, skip_gain.reshape(1, width), w_out,
        jnp.asarray(over), jnp.asarray(spread), jnp.asarray(turns), jnp.asarray(waves),
    )
    kept, crossed = pl.pallas_call(
        functools.partial(kernel, n_ctx, n_fft, group_size),
        out_shape=(jax.ShapeDtypeStruct((piece, width), BF16), jax.ShapeDtypeStruct((piece, width), BF16)),
        in_specs=[pl.BlockSpec(memory_space=pl.ANY)] * len(args),
        out_specs=(pl.BlockSpec(memory_space=pl.ANY), pl.BlockSpec(memory_space=pl.ANY)),
        scratch_shapes=[vmem(a.shape, a.dtype) for a in args] + [
            vmem((rows, 2 * rows), BF16),
            vmem((3, block // lc, tok_len + RIM, lc), F32),
            vmem((tok_len, block), F32),
            vmem((tok_len, block), BF16),
            vmem((n_ctx, stretch, tok_len), BF16),
            vmem((n_ctx, stretch, tok_len), BF16),
            vmem((n_groups, lag_rows, tok_len // lag_rows), BF16),
            vmem((n_ctx, lag_rows, tok_len // lag_rows), BF16),
            vmem((rows, tok_len), BF16),
            vmem((2 * rows, 2 * tok_len), BF16),
            vmem((2 * rows, 2 * tok_len), BF16),
            vmem((2, n_ctx, tok_len), F32),
            vmem((2 * rows, tok_len // 2), BF16),
            vmem((n_ctx, stretch, tok_len), BF16),
            vmem((n_ctx, stretch, tok_len), BF16),
            vmem((tok_len, block), BF16),
            vmem((n_chunks, tok_len // 2, oc), F32),
            vmem((piece, width), BF16),
            vmem((2 * n_chunks, piece, oc), BF16),
            vmem((2 * n_chunks, piece, oc), BF16),
            vmem((2, n_chunks // 2, piece, oc), BF16),
            vmem((piece, block), BF16),
            vmem((2, piece, block), BF16),
            dma((13,)), dma((3,)), dma((3,)), dma((2,)), dma((2,)), dma((2,)), dma((3,)), dma((3,)),
            dma((2 * n_chunks,)), dma((2 * n_chunks,)), dma((2, n_chunks // 2)), dma((n_chunks,)), dma((2, 2)),
        ],
        compiler_params=pltpu.CompilerParams(
            collective_id=0, has_side_effects=True, vmem_limit_bytes=60 * 1024 * 1024
        ),
        name="hyena",
    )(*args)
    return (kept.astype(F32) + crossed.astype(F32)).astype(BF16)


def solution(mesh):
    return jax.shard_map(
        body,
        mesh=mesh,
        in_specs=(P("ctx", None), P(None, None, "fft"), P(), P("ctx", None), P(), P("fft", None)),
        out_specs=P(("ctx", "fft"), None),
        check_vma=False,
    )
```
